1024 devices in a mesh: section: 32 (over z, x_lo), dp: 16 (over y, x_hi), tensor: 2 (over core).
Axes of the slice: x: 8 (x_hi: 2, x_lo: 4; x = x_hi * 4 + x_lo), y: 8, z: 8, core: 2. Of those that a mesh axis runs over, the one named last changes fastest.
Arguments:
- tokens: bfloat16 [32, 2048, 4096], P('section', 'dp', 'tensor'), may hold values from -6 to 6
- lengths: int32 [32, 16], P(None, 'dp'), may hold values from 16 to 128, as said below
- w_query: bfloat16 [32, 4096, 256], P('section', None, 'tensor')
- w_key: bfloat16 [32, 4096, 256], P('section', None, 'tensor')
- w_value: bfloat16 [32, 4096, 256], P('section', None, 'tensor'), may hold values from -0.09375 to 0.09375
- w_out: bfloat16 [32, 256, 4096], P('section', 'tensor'), may hold values from -0.375 to 0.375
- w_embed: bfloat16 [4096, 1024], P('tensor'), may hold values from -0.09375 to 0.09375
Outputs:
- penalty_grad: float32 [32, 2048, 1024], P('section', 'dp', 'tensor')
The draws below stay inside these ranges and needn't reach their ends.
Inputs may be any that keep to these rules, and one draw needn't show every extreme that they name: `lengths`: every length is at least 16; at least one length equals 128.
All inputs are finite; a program needn't handle non-finite values.
Results may differ from the reference program's by a relative error of at most 0.02.
Values may be sent and summed in bfloat16 or wider, within the bound.
A program may use at most 32 MiB of HBM per device.

```python
import math
import jax
import jax.numpy as jnp
from jax import lax

D = 4096
HD = 128
HEADS = 2
E = 1024
HOPS = 2
SEQ = 128
SECTIONS = 32
GROUPS = 16
ROWS = 2048
HW = 256
N_TENSOR = 2


def query_key_pair(key):
    shape = (SECTIONS, D, HW)
    base_key = jax.random.normal(jax.random.fold_in(key, 11), shape, jnp.float32) / jnp.sqrt(jnp.float32(D))
    base_query = jax.random.normal(jax.random.fold_in(key, 12), shape, jnp.float32) / jnp.sqrt(jnp.float32(D))
    queries = base_query
    return (queries, base_key)


def draw_w_query(key, part):
    return query_key_pair(key)[0].astype(jnp.bfloat16)


def draw_w_key(key, part):
    return query_key_pair(key)[1].astype(jnp.bfloat16)


def draw_lengths(key, part):
    drawn = jax.random.randint(jax.random.fold_in(key, 21), (SECTIONS * GROUPS,), SEQ // 8, SEQ + 1)
    chosen = jax.random.randint(jax.random.fold_in(key, 22), (), 0, SECTIONS * GROUPS)
    flat = jnp.where(jnp.arange(SECTIONS * GROUPS) == chosen, SEQ, drawn)
    return flat.reshape(SECTIONS, GROUPS).astype(jnp.int32)


def levels(rng, dims, cuts, low, top_value):
    level, own = 1.0, jax.random.fold_in(rng, 6)
    for axis_at, shards_of in cuts:
        draws = jnp.exp(jax.random.uniform(jax.random.fold_in(own, axis_at), (shards_of,), jnp.float32, low / len(cuts), top_value / len(cuts)))
        level = level * jnp.repeat(draws, dims[axis_at] // shards_of).reshape([-1 if axis == axis_at else 1 for axis in range(len(dims))])
    return level


def bell_draw(rng, extent, deviation, bound, cuts=(), kind=jnp.bfloat16):
    values = deviation * jax.random.normal(rng, extent, jnp.float32)
    if cuts:
        values = values * levels(rng, extent, cuts, -0.22, 0.18)
    return jnp.clip(values, -bound, bound).astype(kind)


def setup_inputs(seed: int = 0) -> dict:
    arg_keys = jax.random.split(jax.random.key(seed), 8)
    tokens = bell_draw(arg_keys[0], (SECTIONS, ROWS, D), 1.0, 6.0, ((0, 32), (1, 16), (2, 2)))
    lengths = draw_lengths(jax.random.fold_in(arg_keys[7], 71), 0)
    w_query = draw_w_query(jax.random.fold_in(arg_keys[7], 71), 0)
    w_key = draw_w_key(jax.random.fold_in(arg_keys[7], 71), 0)
    w_value = bell_draw(arg_keys[4], (SECTIONS, D, HW), D ** -0.5, 0.09375, ((0, 32), (2, 2)))
    w_out = bell_draw(arg_keys[5], (SECTIONS, HW, D), HW ** -0.5, 0.375, ((0, 32), (1, 2)))
    w_embed = bell_draw(arg_keys[6], (D, E), D ** -0.5, 0.09375, ((0, 2),))
    return {"tokens": tokens, "lengths": lengths, "w_query": w_query, "w_key": w_key, "w_value": w_value, "w_out": w_out, "w_embed": w_embed}


EPSILON = 1e-05

def layer_step(state, w_query, w_key, w_value, w_out, group_lens):
    values32 = state.astype(jnp.float32)
    normed = (values32 * lax.rsqrt(lax.optimization_barrier(jnp.mean(values32 * values32, axis=-1, keepdims=True)) + EPSILON)).astype(jnp.bfloat16)
    query_rows = jnp.dot(normed, w_query, preferred_element_type=jnp.float32).astype(jnp.bfloat16)
    key_rows = jnp.dot(normed, w_key, preferred_element_type=jnp.float32).astype(jnp.bfloat16)
    value_rows = jnp.dot(normed, w_value, preferred_element_type=jnp.float32).astype(jnp.bfloat16)
    query_h = query_rows.reshape(GROUPS, SEQ, HEADS, HD).astype(jnp.float32)
    key_h = key_rows.reshape(GROUPS, SEQ, HEADS, HD).astype(jnp.float32)
    value_h = value_rows.reshape(GROUPS, SEQ, HEADS, HD).astype(jnp.float32)
    scores = jnp.einsum('gqhd,gkhd->ghqk', query_h, key_h) * (1.0 / math.sqrt(HD))
    positions = jnp.arange(SEQ, dtype=jnp.int32)
    key_mask = positions[None, None, None, :] < group_lens[:, None, None, None]
    scores = jnp.where(key_mask, scores, -1e+30)
    row_max = lax.optimization_barrier(jnp.max(scores, axis=-1, keepdims=True))
    exp_scores = jnp.exp(scores - row_max)
    attn_probs = (exp_scores / lax.optimization_barrier(jnp.sum(exp_scores, axis=-1, keepdims=True))).astype(jnp.bfloat16)
    mixed = jnp.einsum('ghqk,gkhd->gqhd', attn_probs.astype(jnp.float32), value_h).astype(jnp.bfloat16)
    mixed = mixed.reshape(ROWS, HW)
    group_width = HW // N_TENSOR
    total = jnp.zeros((ROWS, D), jnp.float32)
    for core in range(N_TENSOR):
        lower = core * group_width
        part = jnp.dot(mixed[:, lower:lower + group_width], w_out[lower:lower + group_width], preferred_element_type=jnp.float32)
        total = total + part.astype(jnp.bfloat16).astype(jnp.float32)
    return (values32 + total).astype(jnp.bfloat16)

def reference(tokens, lengths, w_query, w_key, w_value, w_out, w_embed):

    def one_section(dest):
        anchor = (dest - (HOPS - 1)) % SECTIONS
        state = lax.dynamic_index_in_dim(tokens, anchor, 0, keepdims=False)
        group_lens = lax.dynamic_index_in_dim(lengths, anchor, 0, keepdims=False)
        for hop in range(HOPS):
            section_now = (anchor + hop) % SECTIONS
            state = layer_step(state, lax.dynamic_index_in_dim(w_query, section_now, 0, keepdims=False), lax.dynamic_index_in_dim(w_key, section_now, 0, keepdims=False), lax.dynamic_index_in_dim(w_value, section_now, 0, keepdims=False), lax.dynamic_index_in_dim(w_out, section_now, 0, keepdims=False), group_lens)
        feature_width = D // N_TENSOR
        total = jnp.zeros((ROWS, E), jnp.float32)
        for core in range(N_TENSOR):
            lower = core * feature_width
            part = jnp.dot(state[:, lower:lower + feature_width], w_embed[lower:lower + feature_width], preferred_element_type=jnp.float32)
            total = total + part.astype(jnp.bfloat16).astype(jnp.float32)
        embed = total.astype(jnp.bfloat16)
        positions = jnp.arange(SEQ, dtype=jnp.int32)
        row_live = (positions[None, :] < group_lens[:, None]).reshape(ROWS)
        masked = jnp.where(row_live[:, None], embed, jnp.zeros_like(embed))
        grouped = masked.reshape(GROUPS, SEQ, E).astype(jnp.float32)
        partials = jnp.einsum('gse,gsf->gef', grouped, grouped) / float(SEQ * GROUPS)
        moments = lax.optimization_barrier(jnp.sum(partials.astype(jnp.bfloat16).astype(jnp.float32), axis=0))
        penalty = (moments - jnp.eye(E, dtype=jnp.float32)).astype(jnp.bfloat16)
        return jnp.dot(masked, penalty, preferred_element_type=jnp.float32)
    return lax.map(one_section, jnp.arange(SECTIONS, dtype=jnp.int32))
```

```python
import math

import jax
import jax.numpy as jnp
from jax import lax
from jax.experimental import pallas as pl
from jax.experimental.pallas import tpu as pltpu
from jax.sharding import PartitionSpec as P

HD = 128
SEQ = 128
D = 4096
HALF = 2048
E = 1024
EH = 512
CH = 8
CW = HALF // CH
SUB = 2
SROWS = 64 // SUB
SECTIONS = 32
GROUPS = 16
EPSILON = 1e-05
BF = jnp.bfloat16
F32 = jnp.float32

TOK, WOUT, MIX, STATE, RELAY = 0, 1, 2, 4, 4 + CH
EPART, WPART, OUTX, RING = 4 + 2 * CH, 5 + 2 * CH, 6 + 2 * CH, 7 + 2 * CH
REMOTES = RING + 16 * SUB


def dot(a, b):
    return jnp.dot(a, b, preferred_element_type=F32)


def dot_nt(a, b):
    return lax.dot_general(a, b, (((1,), (1,)), ((), ())), preferred_element_type=F32)


def squares(x):
    x32 = x.astype(F32)
    return jnp.sum(x32 * x32, axis=-1, keepdims=True)


def attend(qkv, total_sq, live):
    scale = lax.rsqrt(total_sq * (1.0 / D) + EPSILON)
    q = (qkv[:, :HD] * scale).astype(BF)
    k = (qkv[:, HD : 2 * HD] * scale).astype(BF)
    v = (qkv[:, 2 * HD :] * scale).astype(BF)
    scores = dot_nt(q, k) * (1.0 / math.sqrt(HD))
    positions = lax.broadcasted_iota(jnp.int32, (SEQ, SEQ), 1)
    scores = jnp.where(positions < live, scores, -1e30)
    weights = jnp.exp(scores - jnp.max(scores, axis=-1, keepdims=True))
    total = jnp.sum(weights, axis=-1, keepdims=True)
    return (dot(weights.astype(BF), v) / total).astype(BF)


def kernel(
    tok, lens, wq, wk, wv, wo, wemb, out,
    x1, w, wob, we, sb, x2, mx, es, er, wes, wer, eo, eg, acc, outr,
    lsem, ssem, rsem,
):
    s = lax.axis_index("section")
    g = lax.axis_index("dp")
    c = lax.axis_index("tensor")
    o = 1 - c
    y, xh = g // 2, lax.rem(g, 2)
    nxt = lax.rem(s + 1, SECTIONS)
    prv = lax.rem(s + SECTIONS - 1, SECTIONS)
    pair = (s, g, o)
    after = (nxt, g, c)
    before = (prv, g, c)
    up = (s, lax.rem(y + 1, 8) * 2 + xh, c)
    down = (s, lax.rem(y + 7, 8) * 2 + xh, c)
    across = (s, y * 2 + 1 - xh, c)

    def local(i, src, dst):
        return pltpu.make_async_copy(src, dst, lsem.at[i])

    def remote(i, src, dst, device):
        return pltpu.make_async_remote_copy(
            src_ref=src, dst_ref=dst, send_sem=ssem.at[i], recv_sem=rsem.at[i],
            device_id=device, device_id_type=pl.DeviceIdType.MESH,
        )

    loads = [local(0, tok.at[0], x1.at[c])]
    for h in range(2):
        for j, ref in enumerate((wq, wk, wv)):
            loads.append(local(
                1 + 3 * h + j,
                ref.at[0, h * HALF : (h + 1) * HALF, :],
                w.at[h, :, j * HD : (j + 1) * HD],
            ))
    loads.append(local(7, wo.at[0, :, pl.ds(pl.multiple_of(c * HALF, HALF), HALF)], wob.at[c]))
    loads.append(local(8, wemb, we))
    for copy in loads:
        copy.start()

    barrier = pltpu.get_barrier_semaphore()
    for device in (pair, after, before, up, down, across):
        pl.semaphore_signal(barrier, inc=1, device_id=device, device_id_type=pl.DeviceIdType.MESH)
    pl.semaphore_wait(barrier, 6)

    send_tok = remote(TOK, tok.at[0], x1.at[c], pair)
    send_tok.start()
    send_wo = remote(
        WOUT, wo.at[0, :, pl.ds(pl.multiple_of(o * HALF, HALF), HALF)], wob.at[c], pair
    )
    send_wo.start()
    sends = [send_tok, send_wo]

    for copy in loads[:7]:
        copy.wait()
    own = x1[c]
    qkv = dot(own, w[c])
    total_sq = squares(own)
    send_tok.wait_recv()
    other = x1[o]
    qkv = qkv + dot(other, w[o])
    total_sq = total_sq + squares(other)
    mx[0, c] = attend(qkv, total_sq, lens[s, 0])
    send = remote(MIX, mx.at[0, c], mx.at[0, c], pair)
    send.start()
    sends.append(send)
    loads[7].wait()
    send_wo.wait_recv()
    send.wait_recv()

    mix0, mix1 = mx[0, 0], mx[0, 1]
    shifts = []
    for j in range(CH):
        cols = slice(j * CW, (j + 1) * CW)
        update = dot(mix0, wob[0, :, cols]) + dot(mix1, wob[1, :, cols])
        sb[j] = (x1[c, :, cols].astype(F32) + update).astype(BF)
        send = remote(STATE + j, sb.at[j], x2.at[c, j], after)
        send.start()
        shifts.append(send)
    sends += shifts

    loads[8].wait()
    wes[0] = dot(wob[0], we[...]).astype(BF)
    wes[1] = dot(wob[1], we[...]).astype(BF)
    send_we = remote(WPART, wes, wer, pair)
    send_we.start()
    sends.append(send_we)

    qkv = jnp.zeros((SEQ, 3 * HD), F32)
    total_sq = jnp.zeros((SEQ, 1), F32)
    epart = jnp.zeros((SEQ, E), F32)
    relays = []
    for j in range(CH):
        rows = slice(j * CW, (j + 1) * CW)
        shifts[j].wait_recv()
        relay = remote(RELAY + j, x2.at[c, j], x2.at[c, j], pair)
        relay.start()
        relays.append(relay)
        part = x2[c, j]
        qkv = qkv + dot(part, w[c, rows, :])
        total_sq = total_sq + squares(part)
        epart = epart + dot(part, we[rows, :])
    sends += relays
    es[...] = epart.astype(BF)
    send_e = remote(EPART, es, er, pair)
    send_e.start()
    sends.append(send_e)
    for j in range(CH):
        relays[j].wait_recv()
        part = x2[o, j]
        qkv = qkv + dot(part, w[o, j * CW : (j + 1) * CW, :])
        total_sq = total_sq + squares(part)
    live = lens[prv, 0]
    mx[1, c] = attend(qkv, total_sq, live)
    send = remote(MIX + 1, mx.at[1, c], mx.at[1, c], pair)
    send.start()
    sends.append(send)

    send_we.wait_recv()
    wfull = [(wes[h].astype(F32) + wer[h].astype(F32)).astype(BF) for h in range(2)]
    send_e.wait_recv()
    base = es[...].astype(F32) + er[...].astype(F32)
    send.wait_recv()
    embed = base + dot(mx[1, 0], wfull[0]) + dot(mx[1, 1], wfull[1])
    row_ids = lax.broadcasted_iota(jnp.int32, (SEQ, E), 0)
    eo[...] = jnp.where(row_ids < live, embed, 0.0).astype(BF)
    for q in range(SUB):
        eg[0, q] = eo[pl.ds(pl.multiple_of(c * 64 + q * SROWS, SROWS), SROWS), :]

    def hop(col, source, target, q, device):
        i = RING + (col * 8 + target) * SUB + q
        src = eg.at[source, q] if target == 0 else eg.at[col * 8 + source, q]
        send = remote(i, src, eg.at[col * 8 + target, q], device)
        send.start()
        sends.append(send)
        return send

    arrive = {}

    def launch(col, slot, q):
        plus, minus = (4, 3) if col == 0 else (3, 4)
        if slot < plus:
            arrive[col, slot + 1, q] = hop(col, slot, slot + 1, q, up)
        if slot == 0 or slot > 8 - minus:
            prior = 7 if slot == 0 else slot - 1
            arrive[col, prior, q] = hop(col, slot, prior, q, down)

    def launch_own():
        for q in range(SUB):
            launch(0, 0, q)
        for q in range(SUB):
            arrive[1, 0, q] = hop(1, 0, 0, q, across)

    def take(col, slot):
        for q in range(SUB):
            arrive[col, slot, q].wait_recv()
            if slot == 0 or (slot < 4 if col == 0 else slot < 3) or slot > (5 if col == 0 else 4):
                launch(col, slot, q)

    def contract(slots, first=False):
        rows = jnp.concatenate(
            [eg[slot].reshape(64, E) for slot in slots], axis=0
        )
        gram = dot_nt(eo[...], rows).astype(BF)
        for h in range(2):
            term = dot(gram, rows[:, h * EH : (h + 1) * EH])
            acc[h] = term if first else acc[h] + term

    launch_own()
    take(0, 1)
    take(0, 7)
    take(1, 0)
    contract([0, 1, 7, 8], True)
    take(0, 2)
    take(0, 6)
    take(1, 1)
    take(1, 7)
    contract([2, 6, 9, 15])
    take(0, 3)
    take(0, 5)
    take(1, 2)
    take(1, 6)
    contract([3, 5, 10, 14])
    take(0, 4)
    take(1, 3)
    take(1, 5)
    take(1, 4)
    contract([4, 11, 13, 12])

    send = remote(OUTX, acc.at[o], outr, pair)
    send.start()
    sends.append(send)
    send.wait_recv()
    half = eo[:, pl.ds(pl.multiple_of(c * EH, EH), EH)].astype(F32)
    out[0] = (acc[c] + outr[...]) * (1.0 / (SEQ * GROUPS)) - half
    for send in sends:
        send.wait_send()


def shards(tokens, lengths, w_query, w_key, w_value, w_out, w_embed):
    anywhere = pl.BlockSpec(memory_space=pl.ANY)
    return pl.pallas_call(
        kernel,
        out_shape=jax.ShapeDtypeStruct((1, SEQ, EH), F32),
        in_specs=[anywhere, pl.BlockSpec(memory_space=pltpu.SMEM)] + [anywhere] * 5,
        out_specs=pl.BlockSpec(memory_space=pltpu.VMEM),
        scratch_shapes=[
            pltpu.VMEM((2, SEQ, HALF), BF),
            pltpu.VMEM((2, HALF, 3 * HD), BF),
            pltpu.VMEM((2, HD, HALF), BF),
            pltpu.VMEM((HALF, E), BF),
            pltpu.VMEM((CH, SEQ, CW), BF),
            pltpu.VMEM((2, CH, SEQ, CW), BF),
            pltpu.VMEM((2, 2, SEQ, HD), BF),
            pltpu.VMEM((SEQ, E), BF),
            pltpu.VMEM((SEQ, E), BF),
            pltpu.VMEM((2, HD, E), BF),
            pltpu.VMEM((2, HD, E), BF),
            pltpu.VMEM((SEQ, E), BF),
            pltpu.VMEM((16, SUB, SROWS, E), BF),
            pltpu.VMEM((2, SEQ, EH), F32),
            pltpu.VMEM((SEQ, EH), F32),
            pltpu.SemaphoreType.DMA((9,)),
            pltpu.SemaphoreType.DMA((REMOTES,)),
            pltpu.SemaphoreType.DMA((REMOTES,)),
        ],
        compiler_params=pltpu.CompilerParams(
            collective_id=0, has_side_effects=True, vmem_limit_bytes=60 * 1024 * 1024
        ),
    )(tokens, lengths, w_query, w_key, w_value, w_out, w_embed)


def solution(mesh):
    return jax.shard_map(
        shards,
        mesh=mesh,
        in_specs=(
            P("section", "dp", "tensor"),
            P(None, "dp"),
            P("section", None, "tensor"),
            P("section", None, "tensor"),
            P("section", None, "tensor"),
            P("section", "tensor", None),
            P("tensor", None),
        ),
        out_specs=P("section", "dp", "tensor"),
        check_vma=False,
    )
```

```python
import math

import jax
import jax.numpy as jnp
from jax import lax
from jax.experimental import pallas as pl
from jax.experimental.pallas import tpu as pltpu
from jax.sharding import PartitionSpec as P

HD = 128
SEQ = 128
D = 4096
HALF = 2048
E = 1024
EH = 512
CH = 8
CW = HALF // CH
SUB = 2
SROWS = 64 // SUB
SECTIONS = 32
GROUPS = 16
EPSILON = 1e-05
BF = jnp.bfloat16
F32 = jnp.float32

TOK, WOUT, MIX, STATE, RELAY = 0, 1, 2, 4, 4 + CH
EPART, WPART, OUTX, RING = 4 + 2 * CH, 5 + 2 * CH, 6 + 2 * CH, 7 + 2 * CH
CROSS = RING + 16 * SUB
REMOTES = CROSS + SUB


def dot(a, b):
    return jnp.dot(a, b, preferred_element_type=F32)


def dot_nt(a, b):
    return lax.dot_general(a, b, (((1,), (1,)), ((), ())), preferred_element_type=F32)


def squares(x):
    x32 = x.astype(F32)
    return jnp.sum(x32 * x32, axis=-1, keepdims=True)


def attend(qkv, total_sq, live):
    scale = lax.rsqrt(total_sq * (1.0 / D) + EPSILON)
    q = (qkv[:, :HD] * scale).astype(BF)
    k = (qkv[:, HD : 2 * HD] * scale).astype(BF)
    v = (qkv[:, 2 * HD :] * scale).astype(BF)
    scores = dot_nt(q, k) * (1.0 / math.sqrt(HD))
    positions = lax.broadcasted_iota(jnp.int32, (SEQ, SEQ), 1)
    scores = jnp.where(positions < live, scores, -1e30)
    weights = jnp.exp(scores - jnp.max(scores, axis=-1, keepdims=True))
    total = jnp.sum(weights, axis=-1, keepdims=True)
    return (dot(weights.astype(BF), v) / total).astype(BF)


def kernel(
    tok, lens, wq, wk, wv, wo, wemb, out,
    x1, w, wob, we, sb, x2, mx, es, er, wes, wer, eo, eg, cross, acc, outr,
    lsem, ssem, rsem,
):
    s = lax.axis_index("section")
    g = lax.axis_index("dp")
    c = lax.axis_index("tensor")
    o = 1 - c
    y, xh = g // 2, lax.rem(g, 2)
    nxt = lax.rem(s + 1, SECTIONS)
    prv = lax.rem(s + SECTIONS - 1, SECTIONS)
    pair = (s, g, o)
    after = (nxt, g, c)
    before = (prv, g, c)
    up = (s, lax.rem(y + 1, 8) * 2 + xh, c)
    down = (s, lax.rem(y + 7, 8) * 2 + xh, c)
    x = xh * 4 + lax.rem(s, 4)
    x_up, x_down = lax.rem(x + 2, 8), lax.rem(x + 6, 8)
    z4 = (s // 4) * 4
    ahead = (z4 + lax.rem(x_up, 4), y * 2 + x_up // 4, c)
    behind = (z4 + lax.rem(x_down, 4), y * 2 + x_down // 4, c)

    def local(i, src, dst):
        return pltpu.make_async_copy(src, dst, lsem.at[i])

    def remote(i, src, dst, device):
        return pltpu.make_async_remote_copy(
            src_ref=src, dst_ref=dst, send_sem=ssem.at[i], recv_sem=rsem.at[i],
            device_id=device, device_id_type=pl.DeviceIdType.MESH,
        )

    loads = [local(0, tok.at[0], x1.at[c])]
    for h in range(2):
        for j, ref in enumerate((wq, wk, wv)):
            loads.append(local(
                1 + 3 * h + j,
                ref.at[0, h * HALF : (h + 1) * HALF, :],
                w.at[h, :, j * HD : (j + 1) * HD],
            ))
    loads.append(local(7, wo.at[0, :, pl.ds(pl.multiple_of(c * HALF, HALF), HALF)], wob.at[c]))
    loads.append(local(8, wemb, we))
    for copy in loads[:7]:
        copy.start()

    barrier = pltpu.get_barrier_semaphore()
    for device in (pair, after, before, up, down, ahead, behind):
        pl.semaphore_signal(barrier, inc=1, device_id=device, device_id_type=pl.DeviceIdType.MESH)
    pl.semaphore_wait(barrier, 7)

    send_tok = remote(TOK, tok.at[0], x1.at[c], pair)
    send_tok.start()
    send_wo = remote(
        WOUT, wo.at[0, :, pl.ds(pl.multiple_of(o * HALF, HALF), HALF)], wob.at[c], pair
    )
    send_wo.start()
    loads[7].start()
    sends = [send_tok, send_wo]

    for copy in loads[:7]:
        copy.wait()
    loads[8].start()
    own = x1[c]
    qkv = dot(own, w[c])
    total_sq = squares(own)
    send_tok.wait_recv()
    other = x1[o]
    qkv = qkv + dot(other, w[o])
    total_sq = total_sq + squares(other)
    mx[0, c] = attend(qkv, total_sq, lens[0, s])
    send = remote(MIX, mx.at[0, c], mx.at[0, c], pair)
    send.start()
    sends.append(send)
    loads[7].wait()
    send_wo.wait_recv()
    send.wait_recv()

    mix0, mix1 = mx[0, 0], mx[0, 1]
    shifts = []
    for j in range(CH):
        cols = slice(j * CW, (j + 1) * CW)
        update = dot(mix0, wob[0, :, cols]) + dot(mix1, wob[1, :, cols])
        sb[j] = (x1[c, :, cols].astype(F32) + update).astype(BF)
        send = remote(STATE + j, sb.at[j], x2.at[c, j], after)
        send.start()
        shifts.append(send)
    sends += shifts

    loads[8].wait()
    wes[0] = dot(wob[0], we[...]).astype(BF)
    wes[1] = dot(wob[1], we[...]).astype(BF)
    send_we = remote(WPART, wes, wer, pair)
    send_we.start()
    sends.append(send_we)

    qkv = jnp.zeros((SEQ, 3 * HD), F32)
    total_sq = jnp.zeros((SEQ, 1), F32)
    epart = jnp.zeros((SEQ, E), F32)
    relays = []
    for j in range(CH):
        rows = slice(j * CW, (j + 1) * CW)
        shifts[j].wait_recv()
        relay = remote(RELAY + j, x2.at[c, j], x2.at[c, j], pair)
        relay.start()
        relays.append(relay)
        part = x2[c, j]
        qkv = qkv + dot(part, w[c, rows, :])
        total_sq = total_sq + squares(part)
        epart = epart + dot(part, we[rows, :])
    sends += relays
    es[...] = epart.astype(BF)
    send_e = remote(EPART, es, er, pair)
    send_e.start()
    sends.append(send_e)
    for j in range(CH):
        relays[j].wait_recv()
        part = x2[o, j]
        qkv = qkv + dot(part, w[o, j * CW : (j + 1) * CW, :])
        total_sq = total_sq + squares(part)
    live = lens[0, prv]
    mx[1, c] = attend(qkv, total_sq, live)
    send = remote(MIX + 1, mx.at[1, c], mx.at[1, c], pair)
    send.start()
    sends.append(send)

    send_we.wait_recv()
    wfull = [(wes[h].astype(F32) + wer[h].astype(F32)).astype(BF) for h in range(2)]
    send_e.wait_recv()
    base = es[...].astype(F32) + er[...].astype(F32)
    send.wait_recv()
    embed = base + dot(mx[1, 0], wfull[0]) + dot(mx[1, 1], wfull[1])
    row_ids = lax.broadcasted_iota(jnp.int32, (SEQ, E), 0)
    eo[...] = jnp.where(row_ids < live, embed, 0.0).astype(BF)
    for q in range(SUB):
        eg[0, q] = eo[pl.ds(pl.multiple_of(c * 64 + q * SROWS, SROWS), SROWS), :]

    def hop(col, source, target, q, device):
        i = RING + (col * 8 + target) * SUB + q
        send = remote(i, eg.at[col * 8 + source, q], eg.at[col * 8 + target, q], device)
        send.start()
        sends.append(send)
        return send

    arrive = {}

    def launch(col, slot, q):
        plus, minus = (4, 3) if col == 0 else (3, 4)
        if slot < plus:
            arrive[col, slot + 1, q] = hop(col, slot, slot + 1, q, up)
        if slot == 0 or slot > 8 - minus:
            prior = 7 if slot == 0 else slot - 1
            arrive[col, prior, q] = hop(col, slot, prior, q, down)

    def launch_own():
        for q in range(SUB):
            launch(0, 0, q)
        for q, device in enumerate((ahead, behind)):
            send = remote(CROSS + q, eg.at[0, q], cross.at[q], device)
            send.start()
            sends.append(send)
            arrive["cross", q] = send

    def pass_on():
        for q, device in enumerate((ahead, behind)):
            arrive["cross", q].wait_recv()
            send = remote(RING + 8 * SUB + q, cross.at[q], eg.at[8, q], device)
            send.start()
            sends.append(send)
            arrive[1, 0, q] = send

    def take(col, slot):
        for q in range(SUB):
            arrive[col, slot, q].wait_recv()
            if slot == 0 or (slot < 4 if col == 0 else slot < 3) or slot > (5 if col == 0 else 4):
                launch(col, slot, q)

    def contract(slots, first=False):
        rows = jnp.concatenate(
            [eg[slot].reshape(64, E) for slot in slots], axis=0
        )
        gram = dot_nt(eo[...], rows).astype(BF)
        for h in range(2):
            term = dot(gram, rows[:, h * EH : (h + 1) * EH])
            acc[h] = term if first else acc[h] + term

    launch_own()
    take(0, 1)
    take(0, 7)
    pass_on()
    contract([0, 1, 7], True)
    take(0, 2)
    take(0, 6)
    take(0, 3)
    take(0, 5)
    contract([2, 6, 3, 5])
    take(1, 0)
    take(0, 4)
    take(1, 1)
    take(1, 7)
    contract([4, 8, 9, 15])
    take(1, 2)
    take(1, 6)
    contract([10, 14])
    take(1, 3)
    take(1, 5)
    take(1, 4)
    contract([11, 13, 12])

    send = remote(OUTX, acc.at[o], outr, pair)
    send.start()
    sends.append(send)
    send.wait_recv()
    half = eo[:, pl.ds(pl.multiple_of(c * EH, EH), EH)].astype(F32)
    out[0] = (acc[c] + outr[...]) - half * float(SEQ * GROUPS)
    for send in sends:
        send.wait_send()


def shards(tokens, lengths, w_query, w_key, w_value, w_out, w_embed):
    anywhere = pl.BlockSpec(memory_space=pl.ANY)
    total = pl.pallas_call(
        kernel,
        out_shape=jax.ShapeDtypeStruct((1, SEQ, EH), F32),
        in_specs=[anywhere, pl.BlockSpec(memory_space=pltpu.SMEM)] + [anywhere] * 5,
        out_specs=pl.BlockSpec(memory_space=pltpu.VMEM),
        scratch_shapes=[
            pltpu.VMEM((2, SEQ, HALF), BF),
            pltpu.VMEM((2, HALF, 3 * HD), BF),
            pltpu.VMEM((2, HD, HALF), BF),
            pltpu.VMEM((HALF, E), BF),
            pltpu.VMEM((CH, SEQ, CW), BF),
            pltpu.VMEM((2, CH, SEQ, CW), BF),
            pltpu.VMEM((2, 2, SEQ, HD), BF),
            pltpu.VMEM((SEQ, E), BF),
            pltpu.VMEM((SEQ, E), BF),
            pltpu.VMEM((2, HD, E), BF),
            pltpu.VMEM((2, HD, E), BF),
            pltpu.VMEM((SEQ, E), BF),
            pltpu.VMEM((16, SUB, SROWS, E), BF),
            pltpu.VMEM((SUB, SROWS, E), BF),
            pltpu.VMEM((2, SEQ, EH), F32),
            pltpu.VMEM((SEQ, EH), F32),
            pltpu.SemaphoreType.DMA((9,)),
            pltpu.SemaphoreType.DMA((REMOTES,)),
            pltpu.SemaphoreType.DMA((REMOTES,)),
        ],
        compiler_params=pltpu.CompilerParams(
            collective_id=0, has_side_effects=True, vmem_limit_bytes=60 * 1024 * 1024
        ),
    )(tokens, lengths.reshape(1, SECTIONS), w_query, w_key, w_value, w_out, w_embed)
    return total * (1.0 / (SEQ * GROUPS))


def solution(mesh):
    return jax.shard_map(
        shards,
        mesh=mesh,
        in_specs=(
            P("section", "dp", "tensor"),
            P(None, "dp"),
            P("section", None, "tensor"),
            P("section", None, "tensor"),
            P("section", None, "tensor"),
            P("section", "tensor", None),
            P("tensor", None),
        ),
        out_specs=P("section", "dp", "tensor"),
        check_vma=False,
    )
```

```python
import math

import jax
import jax.numpy as jnp
from jax import lax
from jax.experimental import pallas as pl
from jax.experimental.pallas import tpu as pltpu
from jax.sharding import PartitionSpec as P

HD = 128
SEQ = 128
D = 4096
HALF = 2048
E = 1024
EH = 512
CH = 8
CW = HALF // CH
PART = 64
SECTIONS = 32
GROUPS = 16
EPSILON = 1e-05
BF = jnp.bfloat16
F32 = jnp.float32

FIRST = 3
(TOK, WOUT, MIX, EPART, WPART, ESHIP, EPAIR, ECROSS, EXPAIR, ACROSS, PARTNER, OWN, BACK) = (
    0, 1, 2, 4, 5, 6, 7, 8, 9, 10, 11, 12, 13)
STATE = 14
RELAY = STATE + CH
EGAT = RELAY + CH
AGAT = EGAT + 8
REMOTES = AGAT + 8


def dot(a, b):
    return jnp.dot(a, b, preferred_element_type=F32)


def dot_nt(a, b):
    return lax.dot_general(a, b, (((1,), (1,)), ((), ())), preferred_element_type=F32)


def squares(x):
    x32 = x.astype(F32)
    return jnp.sum(x32 * x32, axis=-1, keepdims=True)


def attend(qkv, total_sq, live):
    scale = lax.rsqrt(total_sq * (1.0 / D) + EPSILON)
    q = (qkv[:, :HD] * scale).astype(BF)
    k = (qkv[:, HD : 2 * HD] * scale).astype(BF)
    v = (qkv[:, 2 * HD :] * scale).astype(BF)
    scores = dot_nt(q, k) * (1.0 / math.sqrt(HD))
    positions = lax.broadcasted_iota(jnp.int32, (SEQ, SEQ), 1)
    scores = jnp.where(positions < live, scores, -1e30)
    weights = jnp.exp(scores - jnp.max(scores, axis=-1, keepdims=True))
    total = jnp.sum(weights, axis=-1, keepdims=True)
    return (dot(weights.astype(BF), v) / total).astype(BF)


def kernel(
    tok, lens, wq, wk, wv, wo, wemb, out,
    x1, w, wob, we, sb, x2, mx, es, er, e1s, e1, xe1, eg, ag, xmx, wes, wer, acc, got, back, gotb,
    lsem, ssem, rsem,
):
    s = lax.axis_index("section")
    g = lax.axis_index("dp")
    c = lax.axis_index("tensor")
    o = 1 - c
    y, xh = g // 2, lax.rem(g, 2)
    nxt = lax.rem(s + 1, SECTIONS)
    prv = lax.rem(s + SECTIONS - 1, SECTIONS)
    pair = (s, g, o)
    after = (nxt, g, c)
    before = (prv, g, c)
    across = (s, y * 2 + 1 - xh, c)
    peers = {d: (s, lax.rem(y + d, 8) * 2 + xh, c) for d in (4, 3, 5, 2, 6, 1, 7)}

    def local(i, src, dst):
        return pltpu.make_async_copy(src, dst, lsem.at[i])

    def remote(i, src, dst, device):
        return pltpu.make_async_remote_copy(
            src_ref=src, dst_ref=dst, send_sem=ssem.at[i], recv_sem=rsem.at[i],
            device_id=device, device_id_type=pl.DeviceIdType.MESH,
        )

    loads = [local(0, tok.at[0], x1.at[c])]
    for h in range(2):
        for j, ref in enumerate((wq, wk, wv)):
            loads.append(local(
                1 + 3 * h + j,
                ref.at[0, h * HALF : (h + 1) * HALF, :],
                w.at[h, :, j * HD : (j + 1) * HD],
            ))
    loads.append(local(7, wo.at[0, :, pl.ds(pl.multiple_of(c * HALF, HALF), HALF)], wob.at[c]))
    loads.append(local(8, wemb, we))
    for copy in loads[:7]:
        copy.start()

    barrier = pltpu.get_barrier_semaphore()
    for device in (pair, after, before, across, *peers.values()):
        pl.semaphore_signal(barrier, inc=1, device_id=device, device_id_type=pl.DeviceIdType.MESH)
    pl.semaphore_wait(barrier, 11)

    send_tok = remote(TOK, tok.at[0], x1.at[c], pair)
    send_tok.start()
    send_wo = remote(
        WOUT, wo.at[0, :, pl.ds(pl.multiple_of(o * HALF, HALF), HALF)], wob.at[c], pair
    )
    send_wo.start()
    loads[7].start()
    sends = [send_tok, send_wo]

    for copy in loads[:7]:
        copy.wait()
    loads[8].start()
    own = x1[c]
    qkv = dot(own, w[c])
    total_sq = squares(own)
    send_tok.wait_recv()
    other = x1[o]
    qkv = qkv + dot(other, w[o])
    total_sq = total_sq + squares(other)
    mx[0, c] = attend(qkv, total_sq, lens[0, s])
    send = remote(MIX, mx.at[0, c], mx.at[0, c], pair)
    send.start()
    sends.append(send)
    loads[7].wait()
    send_wo.wait_recv()
    send.wait_recv()

    def start(i, src, dst, device):
        copy = remote(i, src, dst, device)
        copy.start()
        sends.append(copy)
        return copy

    loads[8].wait()
    mix0, mix1 = mx[0, 0], mx[0, 1]
    epart = jnp.zeros((SEQ, E), F32)
    shifts = [None] * CH
    for j in range(CH):
        cols = slice(j * CW, (j + 1) * CW)
        update = dot(mix0, wob[0, :, cols]) + dot(mix1, wob[1, :, cols])
        part = (x1[c, :, cols].astype(F32) + update).astype(BF)
        sb[j] = part
        if j < FIRST:
            shifts[j] = start(STATE + j, sb.at[j], x2.at[c, j], after)
        epart = epart + dot(part, we[cols, :])
    es[0] = epart[:PART].astype(BF)
    es[1] = epart[PART:].astype(BF)
    send_e = start(EPART, es.at[o], er, pair)
    wes[0] = dot(wob[0], we[...]).astype(BF)
    wes[1] = dot(wob[1], we[...]).astype(BF)
    send_e.wait_recv()
    row_ids = c * PART + lax.broadcasted_iota(jnp.int32, (PART, E), 0)
    mine = es[c].astype(F32) + er[...].astype(F32)
    e1s[...] = jnp.where(row_ids < lens[0, s], mine, 0.0).astype(BF)
    ship = start(ESHIP, e1s, e1.at[c], after)
    for j in range(FIRST, CH):
        shifts[j] = start(STATE + j, sb.at[j], x2.at[c, j], after)
    send_we = start(WPART, wes, wer, pair)

    qkv = jnp.zeros((SEQ, 3 * HD), F32)
    total_sq = jnp.zeros((SEQ, 1), F32)
    relays = []
    gather_e, gather_a = {}, {}
    for j in range(CH):
        if j == FIRST:
            ship.wait_recv()
            e_pair = start(EPAIR, e1.at[c], e1.at[c], pair)
            for d, device in peers.items():
                gather_e[d] = start(EGAT + d, e1.at[c], eg.at[d], device)
        rows = slice(j * CW, (j + 1) * CW)
        shifts[j].wait_recv()
        relays.append(start(RELAY + j, x2.at[c, j], x2.at[c, j], pair))
        part = x2[c, j]
        qkv = qkv + dot(part, w[c, rows, :])
        total_sq = total_sq + squares(part)
    e_cross = start(ECROSS, e1.at[c], xe1.at[c], across)
    for j in range(CH):
        relays[j].wait_recv()
        part = x2[o, j]
        qkv = qkv + dot(part, w[o, j * CW : (j + 1) * CW, :])
        total_sq = total_sq + squares(part)
    live = lens[0, prv]
    mixed = attend(qkv, total_sq, live)
    mixed_rows = lax.broadcasted_iota(jnp.int32, (SEQ, HD), 0)
    mx[1, c] = jnp.where(mixed_rows < live, mixed.astype(F32), 0.0).astype(BF)
    send = start(MIX + 1, mx.at[1, c], mx.at[1, c], pair)
    send.wait_recv()
    own_rows = pl.ds(pl.multiple_of(c * PART, PART), PART)
    for d, device in peers.items():
        gather_a[d] = start(AGAT + d, mx.at[1, :, own_rows, :], ag.at[d], device)
    a_cross = start(ACROSS, mx.at[1], xmx, across)

    send_we.wait_recv()
    full = jnp.concatenate(
        [(wes[h].astype(F32) + wer[h].astype(F32)).astype(BF) for h in range(2)], axis=0
    )

    def embed(first, heads):
        heads = jnp.concatenate([heads[0], heads[1]], axis=1)
        return (first.astype(F32) + dot(heads, full)).astype(BF)

    e_pair.wait_recv()
    own = embed(e1[...].reshape(SEQ, E), mx[1])
    e_cross.wait_recv()
    ex_pair = start(EXPAIR, xe1.at[c], xe1.at[c], pair)
    a_cross.wait_recv()
    ex_pair.wait_recv()
    partner = embed(xe1[...].reshape(SEQ, E), xmx[...])
    both = jnp.concatenate([partner, own], axis=0)

    def pieces(slots):
        firsts = jnp.concatenate([e1[c] if d == 0 else eg[d] for d in slots], axis=0)
        heads = [
            jnp.concatenate(
                [mx[1, h, own_rows, :] if d == 0 else ag[d, h] for d in slots], axis=0
            )
            for h in range(2)
        ]
        return embed(firsts, heads)

    total = None
    for slots in ((0, 1, 7, 2), (6, 3, 5, 4)):
        for d in slots:
            if d:
                gather_e[d].wait_recv()
                gather_a[d].wait_recv()
        rows = pieces(slots)
        gram = dot_nt(both, rows).astype(BF)
        for n in range(4):
            h, m = n % 2, n // 2
            term = dot(gram[m * SEQ : (m + 1) * SEQ], rows[:, h * EH : (h + 1) * EH])
            if slots[0] == 0:
                acc[m, h] = term
            else:
                acc[m, h] = acc[m, h] + term
    partner_sum = start(PARTNER, acc.at[0, o], got.at[0], pair)
    own_sum = start(OWN, acc.at[1, o], got.at[1], pair)
    partner_sum.wait_recv()
    back[...] = (acc[0, c] + got[0]).astype(BF)
    give_back = start(BACK, back, gotb, across)
    own_sum.wait_recv()
    acc[1, c] = acc[1, c] + got[1]
    half = jnp.where(c == 0, own[:, :EH].astype(F32), own[:, EH:].astype(F32))
    give_back.wait_recv()
    out[0] = acc[1, c] + gotb[...].astype(F32) - half * float(SEQ * GROUPS)
    for send in sends:
        send.wait_send()


def shards(tokens, lengths, w_query, w_key, w_value, w_out, w_embed):
    anywhere = pl.BlockSpec(memory_space=pl.ANY)
    total = pl.pallas_call(
        kernel,
        out_shape=jax.ShapeDtypeStruct((1, SEQ, EH), F32),
        in_specs=[anywhere, pl.BlockSpec(memory_space=pltpu.SMEM)] + [anywhere] * 5,
        out_specs=pl.BlockSpec(memory_space=pltpu.VMEM),
        scratch_shapes=[
            pltpu.VMEM((2, SEQ, HALF), BF),
            pltpu.VMEM((2, HALF, 3 * HD), BF),
            pltpu.VMEM((2, HD, HALF), BF),
            pltpu.VMEM((HALF, E), BF),
            pltpu.VMEM((CH, SEQ, CW), BF),
            pltpu.VMEM((2, CH, SEQ, CW), BF),
            pltpu.VMEM((2, 2, SEQ, HD), BF),
            pltpu.VMEM((2, PART, E), BF),
            pltpu.VMEM((PART, E), BF),
            pltpu.VMEM((PART, E), BF),
            pltpu.VMEM((2, PART, E), BF),
            pltpu.VMEM((2, PART, E), BF),
            pltpu.VMEM((8, PART, E), BF),
            pltpu.VMEM((8, 2, PART, HD), BF),
            pltpu.VMEM((2, SEQ, HD), BF),
            pltpu.VMEM((2, HD, E), BF),
            pltpu.VMEM((2, HD, E), BF),
            pltpu.VMEM((2, 2, SEQ, EH), F32),
            pltpu.VMEM((2, SEQ, EH), F32),
            pltpu.VMEM((SEQ, EH), BF),
            pltpu.VMEM((SEQ, EH), BF),
            pltpu.SemaphoreType.DMA((9,)),
            pltpu.SemaphoreType.DMA((REMOTES,)),
            pltpu.SemaphoreType.DMA((REMOTES,)),
        ],
        compiler_params=pltpu.CompilerParams(
            collective_id=0, has_side_effects=True, vmem_limit_bytes=60 * 1024 * 1024
        ),
    )(tokens, lengths.reshape(1, SECTIONS), w_query, w_key, w_value, w_out, w_embed)
    return total * (1.0 / (SEQ * GROUPS))


def solution(mesh):
    return jax.shard_map(
        shards,
        mesh=mesh,
        in_specs=(
            P("section", "dp", "tensor"),
            P(None, "dp"),
            P("section", None, "tensor"),
            P("section", None, "tensor"),
            P("section", None, "tensor"),
            P("section", "tensor", None),
            P("tensor", None),
        ),
        out_specs=P("section", "dp", "tensor"),
        check_vma=False,
    )
```

```python
import math

import jax
import jax.numpy as jnp
from jax import lax
from jax.experimental import pallas as pl
from jax.experimental.pallas import tpu as pltpu
from jax.sharding import PartitionSpec as P

HD = 128
SEQ = 128
D = 4096
HALF = 2048
E = 1024
EH = 512
CH = 8
CW = HALF // CH
PART = 64
SECTIONS = 32
GROUPS = 16
EPSILON = 1e-05
BF = jnp.bfloat16
F32 = jnp.float32

FIRST = 2
(TOK, WOUT, MIX, EPART, WPART, ESHIP, EPAIR, ECROSS, EXPAIR, ACROSS, PARTNER, OWN, BACK) = (
    0, 1, 2, 4, 5, 6, 7, 8, 9, 10, 11, 12, 13)
STATE = 14
RELAY = STATE + CH
EGAT = RELAY + CH
AGAT = EGAT + 8
REMOTES = AGAT + 8


def dot(a, b):
    return jnp.dot(a, b, preferred_element_type=F32)


def dot_nt(a, b):
    return lax.dot_general(a, b, (((1,), (1,)), ((), ())), preferred_element_type=F32)


def squares(x):
    x32 = x.astype(F32)
    return jnp.sum(x32 * x32, axis=-1, keepdims=True)


def attend(qkv, total_sq, live):
    scale = lax.rsqrt(total_sq * (1.0 / D) + EPSILON)
    q = (qkv[:, :HD] * scale).astype(BF)
    k = (qkv[:, HD : 2 * HD] * scale).astype(BF)
    v = (qkv[:, 2 * HD :] * scale).astype(BF)
    scores = dot_nt(q, k) * (1.0 / math.sqrt(HD))
    positions = lax.broadcasted_iota(jnp.int32, (SEQ, SEQ), 1)
    scores = jnp.where(positions < live, scores, -1e30)
    weights = jnp.exp(scores - jnp.max(scores, axis=-1, keepdims=True))
    total = jnp.sum(weights, axis=-1, keepdims=True)
    return (dot(weights.astype(BF), v) / total).astype(BF)


def kernel(
    tok, lens, wq, wk, wv, wo, wemb, out,
    x1, w, wob, we, sb, x2, mx, es, er, e1s, e1, xe1, eg, ag, xmx, wes, wer, acc, got, back, gotb,
    lsem, ssem, rsem,
):
    s = lax.axis_index("section")
    g = lax.axis_index("dp")
    c = lax.axis_index("tensor")
    o = 1 - c
    y, xh = g // 2, lax.rem(g, 2)
    nxt = lax.rem(s + 1, SECTIONS)
    prv = lax.rem(s + SECTIONS - 1, SECTIONS)
    pair = (s, g, o)
    after = (nxt, g, c)
    before = (prv, g, c)
    across = (s, y * 2 + 1 - xh, c)
    peers = {d: (s, lax.rem(y + d, 8) * 2 + xh, c) for d in (4, 3, 5, 2, 6, 1, 7)}

    def local(i, src, dst):
        return pltpu.make_async_copy(src, dst, lsem.at[i])

    def remote(i, src, dst, device):
        return pltpu.make_async_remote_copy(
            src_ref=src, dst_ref=dst, send_sem=ssem.at[i], recv_sem=rsem.at[i],
            device_id=device, device_id_type=pl.DeviceIdType.MESH,
        )

    loads = [local(0, tok.at[0], x1.at[c])]
    for h in range(2):
        for j, ref in enumerate((wq, wk, wv)):
            loads.append(local(
                1 + 3 * h + j,
                ref.at[0, h * HALF : (h + 1) * HALF, :],
                w.at[h, :, j * HD : (j + 1) * HD],
            ))
    loads.append(local(7, wo.at[0, :, pl.ds(pl.multiple_of(c * HALF, HALF), HALF)], wob.at[c]))
    loads.append(local(8, wemb, we))
    for copy in loads[:7]:
        copy.start()

    barrier = pltpu.get_barrier_semaphore()
    for device in (pair, after, before, across, *peers.values()):
        pl.semaphore_signal(barrier, inc=1, device_id=device, device_id_type=pl.DeviceIdType.MESH)
    pl.semaphore_wait(barrier, 11)

    send_tok = remote(TOK, tok.at[0], x1.at[c], pair)
    send_tok.start()
    send_wo = remote(
        WOUT, wo.at[0, :, pl.ds(pl.multiple_of(o * HALF, HALF), HALF)], wob.at[c], pair
    )
    send_wo.start()
    loads[7].start()
    sends = [send_tok, send_wo]

    for copy in loads[:7]:
        copy.wait()
    loads[8].start()
    own = x1[c]
    qkv = dot(own, w[c])
    total_sq = squares(own)
    send_tok.wait_recv()
    other = x1[o]
    qkv = qkv + dot(other, w[o])
    total_sq = total_sq + squares(other)
    mx[0, c] = attend(qkv, total_sq, lens[0, s])
    send = remote(MIX, mx.at[0, c], mx.at[0, c], pair)
    send.start()
    sends.append(send)
    loads[7].wait()
    send_wo.wait_recv()
    send.wait_recv()

    def start(i, src, dst, device):
        copy = remote(i, src, dst, device)
        copy.start()
        sends.append(copy)
        return copy

    mix0, mix1 = mx[0, 0], mx[0, 1]
    shifts = [None] * CH
    for j in range(CH):
        cols = slice(j * CW, (j + 1) * CW)
        update = dot(mix0, wob[0, :, cols]) + dot(mix1, wob[1, :, cols])
        part = (x1[c, :, cols].astype(F32) + update).astype(BF)
        sb[j] = part
        if j < FIRST:
            shifts[j] = start(STATE + j, sb.at[j], x2.at[c, j], after)
    loads[8].wait()
    epart = dot(jnp.concatenate([sb[j] for j in range(CH)], axis=1), we[...])
    es[0] = epart[:PART].astype(BF)
    es[1] = epart[PART:].astype(BF)
    send_e = start(EPART, es.at[o], er, pair)
    send_e.wait_recv()
    row_ids = c * PART + lax.broadcasted_iota(jnp.int32, (PART, E), 0)
    mine = es[c].astype(F32) + er[...].astype(F32)
    e1s[...] = jnp.where(row_ids < lens[0, s], mine, 0.0).astype(BF)
    ship = start(ESHIP, e1s, e1.at[c], after)
    for j in range(FIRST, CH):
        shifts[j] = start(STATE + j, sb.at[j], x2.at[c, j], after)
    wes[0] = dot(wob[0], we[...]).astype(BF)
    wes[1] = dot(wob[1], we[...]).astype(BF)
    send_we = start(WPART, wes, wer, pair)

    qkv = jnp.zeros((SEQ, 3 * HD), F32)
    total_sq = jnp.zeros((SEQ, 1), F32)
    relays = []
    gather_e, gather_a = {}, {}
    for j in range(CH):
        if j == FIRST:
            ship.wait_recv()
            e_pair = start(EPAIR, e1.at[c], e1.at[c], pair)
            for d, device in peers.items():
                gather_e[d] = start(EGAT + d, e1.at[c], eg.at[d], device)
        rows = slice(j * CW, (j + 1) * CW)
        shifts[j].wait_recv()
        relays.append(start(RELAY + j, x2.at[c, j], x2.at[c, j], pair))
        part = x2[c, j]
        qkv = qkv + dot(part, w[c, rows, :])
        total_sq = total_sq + squares(part)
    e_cross = start(ECROSS, e1.at[c], xe1.at[c], across)
    for j in range(CH):
        relays[j].wait_recv()
        part = x2[o, j]
        qkv = qkv + dot(part, w[o, j * CW : (j + 1) * CW, :])
        total_sq = total_sq + squares(part)
    live = lens[0, prv]
    mixed = attend(qkv, total_sq, live)
    mixed_rows = lax.broadcasted_iota(jnp.int32, (SEQ, HD), 0)
    mx[1, c] = jnp.where(mixed_rows < live, mixed.astype(F32), 0.0).astype(BF)
    send = start(MIX + 1, mx.at[1, c], mx.at[1, c], pair)
    send.wait_recv()
    own_rows = pl.ds(pl.multiple_of(c * PART, PART), PART)
    for d, device in peers.items():
        gather_a[d] = start(AGAT + d, mx.at[1, :, own_rows, :], ag.at[d], device)
    a_cross = start(ACROSS, mx.at[1], xmx, across)

    send_we.wait_recv()
    full = jnp.concatenate(
        [(wes[h].astype(F32) + wer[h].astype(F32)).astype(BF) for h in range(2)], axis=0
    )

    def embed(first, heads):
        heads = jnp.concatenate([heads[0], heads[1]], axis=1)
        return (first.astype(F32) + dot(heads, full)).astype(BF)

    e_pair.wait_recv()
    own = embed(e1[...].reshape(SEQ, E), mx[1])
    e_cross.wait_recv()
    ex_pair = start(EXPAIR, xe1.at[c], xe1.at[c], pair)
    a_cross.wait_recv()
    ex_pair.wait_recv()
    partner = embed(xe1[...].reshape(SEQ, E), xmx[...])
    both = jnp.concatenate([partner, own], axis=0)

    def pieces(slots):
        firsts = jnp.concatenate([e1[c] if d == 0 else eg[d] for d in slots], axis=0)
        heads = [
            jnp.concatenate(
                [mx[1, h, own_rows, :] if d == 0 else ag[d, h] for d in slots], axis=0
            )
            for h in range(2)
        ]
        return embed(firsts, heads)

    total = None
    for slots in ((0, 1, 7, 2), (6, 3, 5, 4)):
        for d in slots:
            if d:
                gather_e[d].wait_recv()
                gather_a[d].wait_recv()
        rows = pieces(slots)
        gram = dot_nt(both, rows).astype(BF)
        for n in range(4):
            h, m = n % 2, n // 2
            term = dot(gram[m * SEQ : (m + 1) * SEQ], rows[:, h * EH : (h + 1) * EH])
            if slots[0] == 0:
                acc[m, h] = term
            else:
                acc[m, h] = acc[m, h] + term
    partner_sum = start(PARTNER, acc.at[0, o], got.at[0], pair)
    own_sum = start(OWN, acc.at[1, o], got.at[1], pair)
    partner_sum.wait_recv()
    back[...] = (acc[0, c] + got[0]).astype(BF)
    give_back = start(BACK, back, gotb, across)
    own_sum.wait_recv()
    acc[1, c] = acc[1, c] + got[1]
    half = jnp.where(c == 0, own[:, :EH].astype(F32), own[:, EH:].astype(F32))
    give_back.wait_recv()
    out[0] = acc[1, c] + gotb[...].astype(F32) - half * float(SEQ * GROUPS)
    for send in sends:
        send.wait_send()


def shards(tokens, lengths, w_query, w_key, w_value, w_out, w_embed):
    anywhere = pl.BlockSpec(memory_space=pl.ANY)
    total = pl.pallas_call(
        kernel,
        out_shape=jax.ShapeDtypeStruct((1, SEQ, EH), F32),
        in_specs=[anywhere, pl.BlockSpec(memory_space=pltpu.SMEM)] + [anywhere] * 5,
        out_specs=pl.BlockSpec(memory_space=pltpu.VMEM),
        scratch_shapes=[
            pltpu.VMEM((2, SEQ, HALF), BF),
            pltpu.VMEM((2, HALF, 3 * HD), BF),
            pltpu.VMEM((2, HD, HALF), BF),
            pltpu.VMEM((HALF, E), BF),
            pltpu.VMEM((CH, SEQ, CW), BF),
            pltpu.VMEM((2, CH, SEQ, CW), BF),
            pltpu.VMEM((2, 2, SEQ, HD), BF),
            pltpu.VMEM((2, PART, E), BF),
            pltpu.VMEM((PART, E), BF),
            pltpu.VMEM((PART, E), BF),
            pltpu.VMEM((2, PART, E), BF),
            pltpu.VMEM((2, PART, E), BF),
            pltpu.VMEM((8, PART, E), BF),
            pltpu.VMEM((8, 2, PART, HD), BF),
            pltpu.VMEM((2, SEQ, HD), BF),
            pltpu.VMEM((2, HD, E), BF),
            pltpu.VMEM((2, HD, E), BF),
            pltpu.VMEM((2, 2, SEQ, EH), F32),
            pltpu.VMEM((2, SEQ, EH), F32),
            pltpu.VMEM((SEQ, EH), BF),
            pltpu.VMEM((SEQ, EH), BF),
            pltpu.SemaphoreType.DMA((9,)),
            pltpu.SemaphoreType.DMA((REMOTES,)),
            pltpu.SemaphoreType.DMA((REMOTES,)),
        ],
        compiler_params=pltpu.CompilerParams(
            collective_id=0, has_side_effects=True, vmem_limit_bytes=60 * 1024 * 1024
        ),
    )(tokens, lengths.reshape(1, SECTIONS), w_query, w_key, w_value, w_out, w_embed)
    return total * (1.0 / (SEQ * GROUPS))


def solution(mesh):
    return jax.shard_map(
        shards,
        mesh=mesh,
        in_specs=(
            P("section", "dp", "tensor"),
            P(None, "dp"),
            P("section", None, "tensor"),
            P("section", None, "tensor"),
            P("section", None, "tensor"),
            P("section", "tensor", None),
            P("tensor", None),
        ),
        out_specs=P("section", "dp", "tensor"),
        check_vma=False,
    )
```

```python
import math

import jax
import jax.numpy as jnp
from jax import lax
from jax.experimental import pallas as pl
from jax.experimental.pallas import tpu as pltpu
from jax.sharding import PartitionSpec as P

HD = 128
SEQ = 128
D = 4096
HALF = 2048
E = 1024
EH = 512
CH = 8
CW = HALF // CH
PART = 64
SECTIONS = 32
GROUPS = 16
EPSILON = 1e-05
BF = jnp.bfloat16
F32 = jnp.float32

FIRST = 2
(TOK, WOUT, MIX, EPART, WPART, ESHIP, EPAIR, ECROSS, EXPAIR, ACROSS, PARTNER, OWN, BACK) = (
    0, 1, 2, 4, 5, 6, 7, 8, 9, 10, 11, 12, 13)
STATE = 14
RELAY = STATE + CH
EGAT = RELAY + CH
AGAT = EGAT + 16
REMOTES = AGAT + 8


def dot(a, b):
    return jnp.dot(a, b, preferred_element_type=F32)


def dot_nt(a, b):
    return lax.dot_general(a, b, (((1,), (1,)), ((), ())), preferred_element_type=F32)


def squares(x):
    x32 = x.astype(F32)
    return jnp.sum(x32 * x32, axis=-1, keepdims=True)


def attend(qkv, total_sq, live):
    scale = lax.rsqrt(total_sq * (1.0 / D) + EPSILON)
    q = (qkv[:, :HD] * scale).astype(BF)
    k = (qkv[:, HD : 2 * HD] * scale).astype(BF)
    v = (qkv[:, 2 * HD :] * scale).astype(BF)
    scores = dot_nt(q, k) * (1.0 / math.sqrt(HD))
    positions = lax.broadcasted_iota(jnp.int32, (SEQ, SEQ), 1)
    scores = jnp.where(positions < live, scores, -1e30)
    weights = jnp.exp(scores - jnp.max(scores, axis=-1, keepdims=True))
    total = jnp.sum(weights, axis=-1, keepdims=True)
    return (dot(weights.astype(BF), v) / total).astype(BF)


def kernel(
    tok, lens, wq, wk, wv, wo, wemb, out,
    x1, w, wob, we, sb, x2, mx, es, er, e1s, e1, xe1, eg, ag, xmx, wes, wer, acc, got, back, gotb,
    lsem, ssem, rsem,
):
    s = lax.axis_index("section")
    g = lax.axis_index("dp")
    c = lax.axis_index("tensor")
    o = 1 - c
    y, xh = g // 2, lax.rem(g, 2)
    nxt = lax.rem(s + 1, SECTIONS)
    prv = lax.rem(s + SECTIONS - 1, SECTIONS)
    pair = (s, g, o)
    after = (nxt, g, c)
    before = (prv, g, c)
    across = (s, y * 2 + 1 - xh, c)
    peers = {d: (s, lax.rem(y + d, 8) * 2 + xh, c) for d in (4, 3, 5, 2, 6, 1, 7)}

    def local(i, src, dst):
        return pltpu.make_async_copy(src, dst, lsem.at[i])

    def remote(i, src, dst, device):
        return pltpu.make_async_remote_copy(
            src_ref=src, dst_ref=dst, send_sem=ssem.at[i], recv_sem=rsem.at[i],
            device_id=device, device_id_type=pl.DeviceIdType.MESH,
        )

    loads = [local(0, tok.at[0], x1.at[c])]
    for h in range(2):
        for j, ref in enumerate((wq, wk, wv)):
            loads.append(local(
                1 + 3 * h + j,
                ref.at[0, h * HALF : (h + 1) * HALF, :],
                w.at[h, :, j * HD : (j + 1) * HD],
            ))
    loads.append(local(7, wo.at[0, :, pl.ds(pl.multiple_of(c * HALF, HALF), HALF)], wob.at[c]))
    loads.append(local(8, wemb, we))
    for copy in loads[:7]:
        copy.start()

    barrier = pltpu.get_barrier_semaphore()
    for device in (pair, after, before, across, *peers.values()):
        pl.semaphore_signal(barrier, inc=1, device_id=device, device_id_type=pl.DeviceIdType.MESH)
    pl.semaphore_wait(barrier, 11)

    send_tok = remote(TOK, tok.at[0], x1.at[c], pair)
    send_tok.start()
    send_wo = remote(
        WOUT, wo.at[0, :, pl.ds(pl.multiple_of(o * HALF, HALF), HALF)], wob.at[c], pair
    )
    send_wo.start()
    loads[7].start()
    sends = [send_tok, send_wo]

    for copy in loads[:7]:
        copy.wait()
    loads[8].start()
    own = x1[c]
    qkv = dot(own, w[c])
    total_sq = squares(own)
    send_tok.wait_recv()
    other = x1[o]
    qkv = qkv + dot(other, w[o])
    total_sq = total_sq + squares(other)
    mx[0, c] = attend(qkv, total_sq, lens[0, s])
    send = remote(MIX, mx.at[0, c], mx.at[0, c], pair)
    send.start()
    sends.append(send)
    loads[7].wait()
    send_wo.wait_recv()
    send.wait_recv()

    def start(i, src, dst, device):
        copy = remote(i, src, dst, device)
        copy.start()
        sends.append(copy)
        return copy

    mix0, mix1 = mx[0, 0], mx[0, 1]
    shifts = [None] * CH
    for j in range(CH):
        cols = slice(j * CW, (j + 1) * CW)
        update = dot(mix0, wob[0, :, cols]) + dot(mix1, wob[1, :, cols])
        part = (x1[c, :, cols].astype(F32) + update).astype(BF)
        sb[j] = part
        if j < FIRST:
            shifts[j] = start(STATE + j, sb.at[j], x2.at[c, j], after)
    loads[8].wait()
    epart = dot(jnp.concatenate([sb[j] for j in range(CH)], axis=1), we[...])
    es[0] = epart[:PART].astype(BF)
    es[1] = epart[PART:].astype(BF)
    send_e = start(EPART, es.at[o], er, pair)
    send_e.wait_recv()
    row_ids = c * PART + lax.broadcasted_iota(jnp.int32, (PART, E), 0)
    mine = es[c].astype(F32) + er[...].astype(F32)
    e1s[...] = jnp.where(row_ids < lens[0, s], mine, 0.0).astype(BF)
    ship = start(ESHIP, e1s, e1.at[c], after)
    for j in range(FIRST, CH):
        shifts[j] = start(STATE + j, sb.at[j], x2.at[c, j], after)
    wes[0] = dot(wob[0], we[...]).astype(BF)
    wes[1] = dot(wob[1], we[...]).astype(BF)
    send_we = start(WPART, wes, wer, pair)

    qkv = jnp.zeros((SEQ, 3 * HD), F32)
    total_sq = jnp.zeros((SEQ, 1), F32)
    relays = []
    gather_e, gather_a = {}, {}

    def ring(q, src, target, device):
        gather_e[target, q] = start(EGAT + 2 * target + q, src, eg.at[target, q], device)

    def take(slot):
        for q in range(2):
            gather_e[slot, q].wait_recv()
            if slot < 3 or (slot == 3 and q == 0):
                ring(q, eg.at[slot, q], slot + 1, peers[1])
            if slot > 5 or (slot == 5 and q == 1):
                ring(q, eg.at[slot, q], slot - 1, peers[7])

    for j in range(CH):
        if j == FIRST:
            ship.wait_recv()
            e_pair = start(EPAIR, e1.at[c], e1.at[c], pair)
            for q in range(2):
                src = e1.at[c, q * 32 : (q + 1) * 32, :]
                ring(q, src, 1, peers[1])
                ring(q, src, 7, peers[7])
        if j == 6:
            take(1)
            take(7)
        rows = slice(j * CW, (j + 1) * CW)
        shifts[j].wait_recv()
        relays.append(start(RELAY + j, x2.at[c, j], x2.at[c, j], pair))
        part = x2[c, j]
        qkv = qkv + dot(part, w[c, rows, :])
        total_sq = total_sq + squares(part)
    e_cross = start(ECROSS, e1.at[c], xe1.at[c], across)
    for j in range(CH):
        relays[j].wait_recv()
        part = x2[o, j]
        qkv = qkv + dot(part, w[o, j * CW : (j + 1) * CW, :])
        total_sq = total_sq + squares(part)
    live = lens[0, prv]
    mixed = attend(qkv, total_sq, live)
    mixed_rows = lax.broadcasted_iota(jnp.int32, (SEQ, HD), 0)
    mx[1, c] = jnp.where(mixed_rows < live, mixed.astype(F32), 0.0).astype(BF)
    send = start(MIX + 1, mx.at[1, c], mx.at[1, c], pair)
    take(2)
    take(6)
    send.wait_recv()
    own_rows = pl.ds(pl.multiple_of(c * PART, PART), PART)
    for d, device in peers.items():
        gather_a[d] = start(AGAT + d, mx.at[1, :, own_rows, :], ag.at[d], device)
    a_cross = start(ACROSS, mx.at[1], xmx, across)

    send_we.wait_recv()
    full = jnp.concatenate(
        [(wes[h].astype(F32) + wer[h].astype(F32)).astype(BF) for h in range(2)], axis=0
    )

    def embed(first, heads):
        heads = jnp.concatenate([heads[0], heads[1]], axis=1)
        return (first.astype(F32) + dot(heads, full)).astype(BF)

    e_pair.wait_recv()
    own = embed(e1[...].reshape(SEQ, E), mx[1])
    take(3)
    take(5)
    e_cross.wait_recv()
    ex_pair = start(EXPAIR, xe1.at[c], xe1.at[c], pair)
    a_cross.wait_recv()
    ex_pair.wait_recv()
    partner = embed(xe1[...].reshape(SEQ, E), xmx[...])
    both = jnp.concatenate([partner, own], axis=0)

    def pieces(slots):
        firsts = jnp.concatenate([e1[c] if d == 0 else eg[d].reshape(PART, E) for d in slots], axis=0)
        heads = [
            jnp.concatenate(
                [mx[1, h, own_rows, :] if d == 0 else ag[d, h] for d in slots], axis=0
            )
            for h in range(2)
        ]
        return embed(firsts, heads)

    for slots in ((0, 1, 7, 2), (6, 3, 5, 4)):
        for d in slots:
            if d == 4:
                take(4)
            if d:
                gather_a[d].wait_recv()
        rows = pieces(slots)
        gram = dot_nt(both, rows).astype(BF)
        for n in range(4):
            h, m = n % 2, n // 2
            term = dot(gram[m * SEQ : (m + 1) * SEQ], rows[:, h * EH : (h + 1) * EH])
            if slots[0] == 0:
                acc[m, h] = term
            else:
                acc[m, h] = acc[m, h] + term
    partner_sum = start(PARTNER, acc.at[0, o], got.at[0], pair)
    own_sum = start(OWN, acc.at[1, o], got.at[1], pair)
    partner_sum.wait_recv()
    back[...] = (acc[0, c] + got[0]).astype(BF)
    give_back = start(BACK, back, gotb, across)
    own_sum.wait_recv()
    acc[1, c] = acc[1, c] + got[1]
    half = jnp.where(c == 0, own[:, :EH].astype(F32), own[:, EH:].astype(F32))
    give_back.wait_recv()
    out[0] = acc[1, c] + gotb[...].astype(F32) - half * float(SEQ * GROUPS)
    for send in sends:
        send.wait_send()


def shards(tokens, lengths, w_query, w_key, w_value, w_out, w_embed):
    anywhere = pl.BlockSpec(memory_space=pl.ANY)
    total = pl.pallas_call(
        kernel,
        out_shape=jax.ShapeDtypeStruct((1, SEQ, EH), F32),
        in_specs=[anywhere, pl.BlockSpec(memory_space=pltpu.SMEM)] + [anywhere] * 5,
        out_specs=pl.BlockSpec(memory_space=pltpu.VMEM),
        scratch_shapes=[
            pltpu.VMEM((2, SEQ, HALF), BF),
            pltpu.VMEM((2, HALF, 3 * HD), BF),
            pltpu.VMEM((2, HD, HALF), BF),
            pltpu.VMEM((HALF, E), BF),
            pltpu.VMEM((CH, SEQ, CW), BF),
            pltpu.VMEM((2, CH, SEQ, CW), BF),
            pltpu.VMEM((2, 2, SEQ, HD), BF),
            pltpu.VMEM((2, PART, E), BF),
            pltpu.VMEM((PART, E), BF),
            pltpu.VMEM((PART, E), BF),
            pltpu.VMEM((2, PART, E), BF),
            pltpu.VMEM((2, PART, E), BF),
            pltpu.VMEM((8, 2, PART // 2, E), BF),
            pltpu.VMEM((8, 2, PART, HD), BF),
            pltpu.VMEM((2, SEQ, HD), BF),
            pltpu.VMEM((2, HD, E), BF),
            pltpu.VMEM((2, HD, E), BF),
            pltpu.VMEM((2, 2, SEQ, EH), F32),
            pltpu.VMEM((2, SEQ, EH), F32),
            pltpu.VMEM((SEQ, EH), BF),
            pltpu.VMEM((SEQ, EH), BF),
            pltpu.SemaphoreType.DMA((9,)),
            pltpu.SemaphoreType.DMA((REMOTES,)),
            pltpu.SemaphoreType.DMA((REMOTES,)),
        ],
        compiler_params=pltpu.CompilerParams(
            collective_id=0, has_side_effects=True, vmem_limit_bytes=60 * 1024 * 1024
        ),
    )(tokens, lengths.reshape(1, SECTIONS), w_query, w_key, w_value, w_out, w_embed)
    return total * (1.0 / (SEQ * GROUPS))


def solution(mesh):
    return jax.shard_map(
        shards,
        mesh=mesh,
        in_specs=(
            P("section", "dp", "tensor"),
            P(None, "dp"),
            P("section", None, "tensor"),
            P("section", None, "tensor"),
            P("section", None, "tensor"),
            P("section", "tensor", None),
            P("tensor", None),
        ),
        out_specs=P("section", "dp", "tensor"),
        check_vma=False,
    )
```

```python
import math

import jax
import jax.numpy as jnp
from jax import lax
from jax.experimental import pallas as pl
from jax.experimental.pallas import tpu as pltpu
from jax.sharding import PartitionSpec as P

HD = 128
SEQ = 128
D = 4096
HALF = 2048
E = 1024
EH = 512
CH = 8
CW = HALF // CH
PART = 64
SECTIONS = 32
GROUPS = 16
EPSILON = 1e-05
BF = jnp.bfloat16
F32 = jnp.float32

FIRST = 2
(TOK, WOUT, MIX, EPART, WPART, ESHIP, EPAIR, ECROSS, EXPAIR, ACROSS, OWN, PARTNER, BACK) = (
    0, 1, 2, 4, 5, 6, 7, 8, 9, 10, 11, 12, 14)
STATE = 16
RELAY = STATE + CH
EGAT = RELAY + CH
AGAT = EGAT + 16
REMOTES = AGAT + 8


def dot(a, b):
    return jnp.dot(a, b, preferred_element_type=F32)


def dot_nt(a, b):
    return lax.dot_general(a, b, (((1,), (1,)), ((), ())), preferred_element_type=F32)


def squares(x):
    x32 = x.astype(F32)
    return jnp.sum(x32 * x32, axis=-1, keepdims=True)


def attend(qkv, total_sq, live):
    scale = lax.rsqrt(total_sq * (1.0 / D) + EPSILON)
    q = (qkv[:, :HD] * scale).astype(BF)
    k = (qkv[:, HD : 2 * HD] * scale).astype(BF)
    v = (qkv[:, 2 * HD :] * scale).astype(BF)
    scores = dot_nt(q, k) * (1.0 / math.sqrt(HD))
    positions = lax.broadcasted_iota(jnp.int32, (SEQ, SEQ), 1)
    scores = jnp.where(positions < live, scores, -1e30)
    weights = jnp.exp(scores - jnp.max(scores, axis=-1, keepdims=True))
    total = jnp.sum(weights, axis=-1, keepdims=True)
    return (dot(weights.astype(BF), v) / total).astype(BF)


def kernel(
    tok, lens, wq, wk, wv, wo, wemb, out,
    x1, w, wob, we, sb, x2, mx, es, er, e1s, e1, xe1, eg, ag, xmx, wes, wer, acc, got, back, gotb,
    lsem, ssem, rsem,
):
    s = lax.axis_index("section")
    g = lax.axis_index("dp")
    c = lax.axis_index("tensor")
    o = 1 - c
    y, xh = g // 2, lax.rem(g, 2)
    nxt = lax.rem(s + 1, SECTIONS)
    prv = lax.rem(s + SECTIONS - 1, SECTIONS)
    pair = (s, g, o)
    after = (nxt, g, c)
    before = (prv, g, c)
    across = (s, y * 2 + 1 - xh, c)
    peers = {d: (s, lax.rem(y + d, 8) * 2 + xh, c) for d in (4, 3, 5, 2, 6, 1, 7)}

    def local(i, src, dst):
        return pltpu.make_async_copy(src, dst, lsem.at[i])

    def remote(i, src, dst, device):
        return pltpu.make_async_remote_copy(
            src_ref=src, dst_ref=dst, send_sem=ssem.at[i], recv_sem=rsem.at[i],
            device_id=device, device_id_type=pl.DeviceIdType.MESH,
        )

    loads = [local(0, tok.at[0], x1.at[c])]
    for h in range(2):
        for j, ref in enumerate((wq, wk, wv)):
            loads.append(local(
                1 + 3 * h + j,
                ref.at[0, h * HALF : (h + 1) * HALF, :],
                w.at[h, :, j * HD : (j + 1) * HD],
            ))
    loads.append(local(7, wo.at[0, :, pl.ds(pl.multiple_of(c * HALF, HALF), HALF)], wob.at[c]))
    loads.append(local(8, wemb, we))
    for copy in loads[:7]:
        copy.start()

    barrier = pltpu.get_barrier_semaphore()
    for device in (pair, after, before, across, *peers.values()):
        pl.semaphore_signal(barrier, inc=1, device_id=device, device_id_type=pl.DeviceIdType.MESH)
    pl.semaphore_wait(barrier, 11)

    send_tok = remote(TOK, tok.at[0], x1.at[c], pair)
    send_tok.start()
    send_wo = remote(
        WOUT, wo.at[0, :, pl.ds(pl.multiple_of(o * HALF, HALF), HALF)], wob.at[c], pair
    )
    send_wo.start()
    loads[7].start()
    sends = [send_tok, send_wo]

    for copy in loads[:7]:
        copy.wait()
    loads[8].start()
    own = x1[c]
    qkv = dot(own, w[c])
    total_sq = squares(own)
    send_tok.wait_recv()
    other = x1[o]
    qkv = qkv + dot(other, w[o])
    total_sq = total_sq + squares(other)
    mx[0, c] = attend(qkv, total_sq, lens[0, s])
    send = remote(MIX, mx.at[0, c], mx.at[0, c], pair)
    send.start()
    sends.append(send)
    loads[7].wait()
    send_wo.wait_recv()
    send.wait_recv()

    def start(i, src, dst, device):
        copy = remote(i, src, dst, device)
        copy.start()
        sends.append(copy)
        return copy

    mix0, mix1 = mx[0, 0], mx[0, 1]
    shifts = [None] * CH
    for j in range(CH):
        cols = slice(j * CW, (j + 1) * CW)
        update = dot(mix0, wob[0, :, cols]) + dot(mix1, wob[1, :, cols])
        part = (x1[c, :, cols].astype(F32) + update).astype(BF)
        sb[j] = part
        if j < FIRST:
            shifts[j] = start(STATE + j, sb.at[j], x2.at[c, j], after)
    loads[8].wait()
    epart = dot(jnp.concatenate([sb[j] for j in range(CH)], axis=1), we[...])
    es[0] = epart[:PART].astype(BF)
    es[1] = epart[PART:].astype(BF)
    send_e = start(EPART, es.at[o], er, pair)
    send_e.wait_recv()
    row_ids = c * PART + lax.broadcasted_iota(jnp.int32, (PART, E), 0)
    mine = es[c].astype(F32) + er[...].astype(F32)
    e1s[...] = jnp.where(row_ids < lens[0, s], mine, 0.0).astype(BF)
    ship = start(ESHIP, e1s, e1.at[c], after)
    for j in range(FIRST, CH):
        shifts[j] = start(STATE + j, sb.at[j], x2.at[c, j], after)
    wes[0] = dot(wob[0], we[...]).astype(BF)
    wes[1] = dot(wob[1], we[...]).astype(BF)
    send_we = start(WPART, wes, wer, pair)

    qkv = jnp.zeros((SEQ, 3 * HD), F32)
    total_sq = jnp.zeros((SEQ, 1), F32)
    relays = []
    gather_e, gather_a = {}, {}

    def ring(q, src, target, device):
        gather_e[target, q] = start(EGAT + 2 * target + q, src, eg.at[target, q], device)

    def take(slot):
        for q in range(2):
            gather_e[slot, q].wait_recv()
            if slot < 3 or (slot == 3 and q == 0):
                ring(q, eg.at[slot, q], slot + 1, peers[1])
            if slot > 5 or (slot == 5 and q == 1):
                ring(q, eg.at[slot, q], slot - 1, peers[7])

    for j in range(CH):
        if j == FIRST:
            ship.wait_recv()
            e_pair = start(EPAIR, e1.at[c], e1.at[c], pair)
            for q in range(2):
                src = e1.at[c, q * 32 : (q + 1) * 32, :]
                ring(q, src, 1, peers[1])
                ring(q, src, 7, peers[7])
        if j == 5:
            take(1)
            take(7)
        rows = slice(j * CW, (j + 1) * CW)
        shifts[j].wait_recv()
        relays.append(start(RELAY + j, x2.at[c, j], x2.at[c, j], pair))
        part = x2[c, j]
        qkv = qkv + dot(part, w[c, rows, :])
        total_sq = total_sq + squares(part)
    e_cross = start(ECROSS, e1.at[c], xe1.at[c], across)
    take(2)
    take(6)
    for j in range(CH):
        relays[j].wait_recv()
        part = x2[o, j]
        qkv = qkv + dot(part, w[o, j * CW : (j + 1) * CW, :])
        total_sq = total_sq + squares(part)
    live = lens[0, prv]
    mixed = attend(qkv, total_sq, live)
    mixed_rows = lax.broadcasted_iota(jnp.int32, (SEQ, HD), 0)
    mx[1, c] = jnp.where(mixed_rows < live, mixed.astype(F32), 0.0).astype(BF)
    send = start(MIX + 1, mx.at[1, c], mx.at[1, c], pair)
    send.wait_recv()
    own_rows = pl.ds(pl.multiple_of(c * PART, PART), PART)
    for d, device in peers.items():
        gather_a[d] = start(AGAT + d, mx.at[1, :, own_rows, :], ag.at[d], device)
    a_cross = start(ACROSS, mx.at[1], xmx, across)

    send_we.wait_recv()
    full = jnp.concatenate(
        [(wes[h].astype(F32) + wer[h].astype(F32)).astype(BF) for h in range(2)], axis=0
    )

    def embed(first, heads):
        heads = jnp.concatenate([heads[0], heads[1]], axis=1)
        return (first.astype(F32) + dot(heads, full)).astype(BF)

    e_pair.wait_recv()
    own = embed(e1[...].reshape(SEQ, E), mx[1])
    take(3)
    take(5)
    e_cross.wait_recv()
    ex_pair = start(EXPAIR, xe1.at[c], xe1.at[c], pair)
    a_cross.wait_recv()
    ex_pair.wait_recv()
    partner = embed(xe1[...].reshape(SEQ, E), xmx[...])
    both = jnp.concatenate([partner, own], axis=0)

    def pieces(slots):
        firsts = jnp.concatenate([e1[c] if d == 0 else eg[d].reshape(PART, E) for d in slots], axis=0)
        heads = [
            jnp.concatenate(
                [mx[1, h, own_rows, :] if d == 0 else ag[d, h] for d in slots], axis=0
            )
            for h in range(2)
        ]
        return embed(firsts, heads)

    for slots in ((0, 1, 7, 2), (6, 3, 5, 4)):
        for d in slots:
            if d == 4:
                take(4)
            if d:
                gather_a[d].wait_recv()
        rows = pieces(slots)
        gram = dot_nt(both, rows).astype(BF)
        if slots[0] == 0:
            for m in range(2):
                for h in range(2):
                    acc[m, h] = dot(gram[m * SEQ : (m + 1) * SEQ], rows[:, h * EH : (h + 1) * EH])
    partner_sum = []
    for m in range(2):
        part_rows = slice(m * PART, (m + 1) * PART)
        for h in range(2):
            term = dot(gram[part_rows], rows[:, h * EH : (h + 1) * EH])
            acc[0, h, part_rows, :] = acc[0, h, part_rows, :] + term
        partner_sum.append(
            start(PARTNER + m, acc.at[0, o, part_rows, :], got.at[0, part_rows, :], pair)
        )
    for h in range(2):
        acc[1, h] = acc[1, h] + dot(gram[SEQ:], rows[:, h * EH : (h + 1) * EH])
    own_sum = start(OWN, acc.at[1, o], got.at[1], pair)
    give_back = []
    for m in range(2):
        part_rows = slice(m * PART, (m + 1) * PART)
        partner_sum[m].wait_recv()
        back[part_rows, :] = (acc[0, c, part_rows, :] + got[0, part_rows, :]).astype(BF)
        give_back.append(
            start(BACK + m, back.at[part_rows, :], gotb.at[part_rows, :], across)
        )
    own_sum.wait_recv()
    acc[1, c] = acc[1, c] + got[1]
    half = jnp.where(c == 0, own[:, :EH].astype(F32), own[:, EH:].astype(F32))
    for copy in give_back:
        copy.wait_recv()
    out[0] = acc[1, c] + gotb[...].astype(F32) - half * float(SEQ * GROUPS)
    for send in sends:
        send.wait_send()


def shards(tokens, lengths, w_query, w_key, w_value, w_out, w_embed):
    anywhere = pl.BlockSpec(memory_space=pl.ANY)
    total = pl.pallas_call(
        kernel,
        out_shape=jax.ShapeDtypeStruct((1, SEQ, EH), F32),
        in_specs=[anywhere, pl.BlockSpec(memory_space=pltpu.SMEM)] + [anywhere] * 5,
        out_specs=pl.BlockSpec(memory_space=pltpu.VMEM),
        scratch_shapes=[
            pltpu.VMEM((2, SEQ, HALF), BF),
            pltpu.VMEM((2, HALF, 3 * HD), BF),
            pltpu.VMEM((2, HD, HALF), BF),
            pltpu.VMEM((HALF, E), BF),
            pltpu.VMEM((CH, SEQ, CW), BF),
            pltpu.VMEM((2, CH, SEQ, CW), BF),
            pltpu.VMEM((2, 2, SEQ, HD), BF),
            pltpu.VMEM((2, PART, E), BF),
            pltpu.VMEM((PART, E), BF),
            pltpu.VMEM((PART, E), BF),
            pltpu.VMEM((2, PART, E), BF),
            pltpu.VMEM((2, PART, E), BF),
            pltpu.VMEM((8, 2, PART // 2, E), BF),
            pltpu.VMEM((8, 2, PART, HD), BF),
            pltpu.VMEM((2, SEQ, HD), BF),
            pltpu.VMEM((2, HD, E), BF),
            pltpu.VMEM((2, HD, E), BF),
            pltpu.VMEM((2, 2, SEQ, EH), F32),
            pltpu.VMEM((2, SEQ, EH), F32),
            pltpu.VMEM((SEQ, EH), BF),
            pltpu.VMEM((SEQ, EH), BF),
            pltpu.SemaphoreType.DMA((9,)),
            pltpu.SemaphoreType.DMA((REMOTES,)),
            pltpu.SemaphoreType.DMA((REMOTES,)),
        ],
        compiler_params=pltpu.CompilerParams(
            collective_id=0, has_side_effects=True, vmem_limit_bytes=60 * 1024 * 1024
        ),
    )(tokens, lengths.reshape(1, SECTIONS), w_query, w_key, w_value, w_out, w_embed)
    return total * (1.0 / (SEQ * GROUPS))


def solution(mesh):
    return jax.shard_map(
        shards,
        mesh=mesh,
        in_specs=(
            P("section", "dp", "tensor"),
            P(None, "dp"),
            P("section", None, "tensor"),
            P("section", None, "tensor"),
            P("section", None, "tensor"),
            P("section", "tensor", None),
            P("tensor", None),
        ),
        out_specs=P("section", "dp", "tensor"),
        check_vma=False,
    )
```

```python
import math

import jax
import jax.numpy as jnp
from jax import lax
from jax.experimental import pallas as pl
from jax.experimental.pallas import tpu as pltpu
from jax.sharding import PartitionSpec as P

HD = 128
SEQ = 128
D = 4096
HALF = 2048
E = 1024
EH = 512
CH = 8
CW = HALF // CH
PART = 64
SECTIONS = 32
GROUPS = 16
EPSILON = 1e-05
BF = jnp.bfloat16
F32 = jnp.float32

FIRST = 2
(TOK, WOUT, MIX, EPART, WPART, ESHIP, EPAIR, ECROSS, EXPAIR, ACROSS, OWN, PARTNER, BACK) = (
    0, 1, 2, 4, 5, 6, 7, 8, 9, 10, 11, 12, 14)
STATE = 16
RELAY = STATE + CH
EGAT = RELAY + CH
AGAT = EGAT + 16
ACAT = AGAT + 16
REMOTES = ACAT + 2


def dot(a, b):
    return jnp.dot(a, b, preferred_element_type=F32)


def dot_nt(a, b):
    return lax.dot_general(a, b, (((1,), (1,)), ((), ())), preferred_element_type=F32)


def squares(x):
    x32 = x.astype(F32)
    return jnp.sum(x32 * x32, axis=-1, keepdims=True)


def attend(qkv, total_sq, live):
    scale = lax.rsqrt(total_sq * (1.0 / D) + EPSILON)
    q = (qkv[:, :HD] * scale).astype(BF)
    k = (qkv[:, HD : 2 * HD] * scale).astype(BF)
    v = (qkv[:, 2 * HD :] * scale).astype(BF)
    scores = dot_nt(q, k) * (1.0 / math.sqrt(HD))
    positions = lax.broadcasted_iota(jnp.int32, (SEQ, SEQ), 1)
    scores = jnp.where(positions < live, scores, -1e30)
    weights = jnp.exp(scores - jnp.max(scores, axis=-1, keepdims=True))
    total = jnp.sum(weights, axis=-1, keepdims=True)
    return (dot(weights.astype(BF), v) / total).astype(BF)


def kernel(
    tok, lens, wq, wk, wv, wo, wemb, out,
    x1, w, wob, we, sb, x2, mx, es, er, e1s, e1, xe1, eg, ag, xmx, wes, wer, acc, got, back, gotb,
    lsem, ssem, rsem,
):
    s = lax.axis_index("section")
    g = lax.axis_index("dp")
    c = lax.axis_index("tensor")
    o = 1 - c
    y, xh = g // 2, lax.rem(g, 2)
    nxt = lax.rem(s + 1, SECTIONS)
    prv = lax.rem(s + SECTIONS - 1, SECTIONS)
    pair = (s, g, o)
    after = (nxt, g, c)
    before = (prv, g, c)
    across = (s, y * 2 + 1 - xh, c)
    peers = {d: (s, lax.rem(y + d, 8) * 2 + xh, c) for d in (4, 3, 5, 2, 6, 1, 7)}
    facing = [(s, across[1], k) for k in range(2)]
    others = [(s, device[1], k) for device in peers.values() for k in range(2)]

    def local(i, src, dst):
        return pltpu.make_async_copy(src, dst, lsem.at[i])

    def remote(i, src, dst, device, landed=None):
        return pltpu.make_async_remote_copy(
            src_ref=src, dst_ref=dst, send_sem=ssem.at[i], recv_sem=rsem.at[i if landed is None else landed],
            device_id=device, device_id_type=pl.DeviceIdType.MESH,
        )

    loads = [local(0, tok.at[0], x1.at[c])]
    for h in range(2):
        for j, ref in enumerate((wq, wk, wv)):
            loads.append(local(
                1 + 3 * h + j,
                ref.at[0, h * HALF : (h + 1) * HALF, :],
                w.at[h, :, j * HD : (j + 1) * HD],
            ))
    loads.append(local(7, wo.at[0, :, pl.ds(pl.multiple_of(c * HALF, HALF), HALF)], wob.at[c]))
    loads.append(local(8, wemb, we))
    for copy in loads[:7]:
        copy.start()

    barrier = pltpu.get_barrier_semaphore()
    for device in (pair, after, before, *facing, *others):
        pl.semaphore_signal(barrier, inc=1, device_id=device, device_id_type=pl.DeviceIdType.MESH)
    pl.semaphore_wait(barrier, 19)

    send_tok = remote(TOK, tok.at[0], x1.at[c], pair)
    send_tok.start()
    send_wo = remote(
        WOUT, wo.at[0, :, pl.ds(pl.multiple_of(o * HALF, HALF), HALF)], wob.at[c], pair
    )
    send_wo.start()
    loads[7].start()
    sends = [send_tok, send_wo]

    for copy in loads[:7]:
        copy.wait()
    loads[8].start()
    own = x1[c]
    qkv = dot(own, w[c])
    total_sq = squares(own)
    send_tok.wait_recv()
    other = x1[o]
    qkv = qkv + dot(other, w[o])
    total_sq = total_sq + squares(other)
    mx[0, c] = attend(qkv, total_sq, lens[0, s])
    send = remote(MIX, mx.at[0, c], mx.at[0, c], pair)
    send.start()
    sends.append(send)
    loads[7].wait()
    send_wo.wait_recv()
    send.wait_recv()

    def start(i, src, dst, device, landed=None):
        copy = remote(i, src, dst, device, landed)
        copy.start()
        sends.append(copy)
        return copy

    mix0, mix1 = mx[0, 0], mx[0, 1]
    shifts = [None] * CH
    for j in range(CH):
        cols = slice(j * CW, (j + 1) * CW)
        update = dot(mix0, wob[0, :, cols]) + dot(mix1, wob[1, :, cols])
        part = (x1[c, :, cols].astype(F32) + update).astype(BF)
        sb[j] = part
        if j < FIRST:
            shifts[j] = start(STATE + j, sb.at[j], x2.at[c, j], after)
    loads[8].wait()
    epart = dot(jnp.concatenate([sb[j] for j in range(CH)], axis=1), we[...])
    es[0] = epart[:PART].astype(BF)
    es[1] = epart[PART:].astype(BF)
    send_e = start(EPART, es.at[o], er, pair)
    send_e.wait_recv()
    row_ids = c * PART + lax.broadcasted_iota(jnp.int32, (PART, E), 0)
    mine = es[c].astype(F32) + er[...].astype(F32)
    e1s[...] = jnp.where(row_ids < lens[0, s], mine, 0.0).astype(BF)
    ship = start(ESHIP, e1s, e1.at[c], after)
    for j in range(FIRST, CH):
        shifts[j] = start(STATE + j, sb.at[j], x2.at[c, j], after)
    wes[0] = dot(wob[0], we[...]).astype(BF)
    wes[1] = dot(wob[1], we[...]).astype(BF)
    send_we = start(WPART, wes, wer, pair)

    qkv = jnp.zeros((SEQ, 3 * HD), F32)
    total_sq = jnp.zeros((SEQ, 1), F32)
    relays = []
    gather_e = {}

    def ring(q, src, target, device):
        gather_e[target, q] = start(EGAT + 2 * target + q, src, eg.at[target, q], device)

    def take(slot):
        for q in range(2):
            gather_e[slot, q].wait_recv()
            if slot < 3 or (slot == 3 and q == 0):
                ring(q, eg.at[slot, q], slot + 1, peers[1])
            if slot > 5 or (slot == 5 and q == 1):
                ring(q, eg.at[slot, q], slot - 1, peers[7])

    for j in range(CH):
        if j == FIRST:
            ship.wait_recv()
            e_pair = start(EPAIR, e1.at[c], e1.at[c], pair)
            for q in range(2):
                src = e1.at[c, q * 32 : (q + 1) * 32, :]
                ring(q, src, 1, peers[1])
                ring(q, src, 7, peers[7])
        if j == 5:
            take(1)
            take(7)
        rows = slice(j * CW, (j + 1) * CW)
        shifts[j].wait_recv()
        relays.append(start(RELAY + j, x2.at[c, j], x2.at[c, j], pair))
        part = x2[c, j]
        qkv = qkv + dot(part, w[c, rows, :])
        total_sq = total_sq + squares(part)
    e_cross = start(ECROSS, e1.at[c], xe1.at[c], across)
    take(2)
    take(6)
    for j in range(CH):
        relays[j].wait_recv()
        part = x2[o, j]
        qkv = qkv + dot(part, w[o, j * CW : (j + 1) * CW, :])
        total_sq = total_sq + squares(part)
    live = lens[0, prv]
    mixed = attend(qkv, total_sq, live)
    mixed_rows = lax.broadcasted_iota(jnp.int32, (SEQ, HD), 0)
    mx[1, c] = jnp.where(mixed_rows < live, mixed.astype(F32), 0.0).astype(BF)
    send = start(MIX + 1, mx.at[1, c], mx.at[1, c], pair)
    for d, device in peers.items():
        for k in range(2):
            start(
                AGAT + 2 * d + k, mx.at[1, c, k * PART : (k + 1) * PART, :], ag.at[d, c],
                (s, device[1], k), AGAT + 2 * d + c,
            )
    for k in range(2):
        start(ACAT + k, mx.at[1, c], xmx.at[c], facing[k], ACAT + c)
    own_rows = pl.ds(pl.multiple_of(c * PART, PART), PART)

    send_we.wait_recv()
    full = jnp.concatenate(
        [(wes[h].astype(F32) + wer[h].astype(F32)).astype(BF) for h in range(2)], axis=0
    )

    def embed(first, heads):
        heads = jnp.concatenate([heads[0], heads[1]], axis=1)
        return (first.astype(F32) + dot(heads, full)).astype(BF)

    e_pair.wait_recv()
    send.wait_recv()
    own = embed(e1[...].reshape(SEQ, E), mx[1])
    take(3)
    take(5)
    e_cross.wait_recv()
    ex_pair = start(EXPAIR, xe1.at[c], xe1.at[c], pair)
    for h in range(2):
        remote(ACAT + h, xmx.at[h], xmx.at[h], across).wait_recv()
    ex_pair.wait_recv()
    partner = embed(xe1[...].reshape(SEQ, E), xmx[...])
    both = jnp.concatenate([partner, own], axis=0)

    def pieces(slots):
        firsts = jnp.concatenate([e1[c] if d == 0 else eg[d].reshape(PART, E) for d in slots], axis=0)
        heads = [
            jnp.concatenate(
                [mx[1, h, own_rows, :] if d == 0 else ag[d, h] for d in slots], axis=0
            )
            for h in range(2)
        ]
        return embed(firsts, heads)

    for slots in ((0, 1, 7, 2), (6, 3, 5, 4)):
        for d in slots:
            if d == 4:
                take(4)
            if d:
                for h in range(2):
                    remote(AGAT + 2 * d + h, ag.at[d, h], ag.at[d, h], across).wait_recv()
        rows = pieces(slots)
        gram = dot_nt(both, rows).astype(BF)
        if slots[0] == 0:
            for m in range(2):
                for h in range(2):
                    acc[m, h] = dot(gram[m * SEQ : (m + 1) * SEQ], rows[:, h * EH : (h + 1) * EH])
    partner_sum = []
    for m in range(2):
        part_rows = slice(m * PART, (m + 1) * PART)
        for h in range(2):
            term = dot(gram[part_rows], rows[:, h * EH : (h + 1) * EH])
            acc[0, h, part_rows, :] = acc[0, h, part_rows, :] + term
        partner_sum.append(
            start(PARTNER + m, acc.at[0, o, part_rows, :], got.at[0, part_rows, :], pair)
        )
    for h in range(2):
        acc[1, h] = acc[1, h] + dot(gram[SEQ:], rows[:, h * EH : (h + 1) * EH])
    own_sum = start(OWN, acc.at[1, o], got.at[1], pair)
    give_back = []
    for m in range(2):
        part_rows = slice(m * PART, (m + 1) * PART)
        partner_sum[m].wait_recv()
        back[part_rows, :] = (acc[0, c, part_rows, :] + got[0, part_rows, :]).astype(BF)
        give_back.append(
            start(BACK + m, back.at[part_rows, :], gotb.at[part_rows, :], across)
        )
    own_sum.wait_recv()
    acc[1, c] = acc[1, c] + got[1]
    half = jnp.where(c == 0, own[:, :EH].astype(F32), own[:, EH:].astype(F32))
    for copy in give_back:
        copy.wait_recv()
    out[0] = acc[1, c] + gotb[...].astype(F32) - half * float(SEQ * GROUPS)
    for send in sends:
        send.wait_send()


def shards(tokens, lengths, w_query, w_key, w_value, w_out, w_embed):
    anywhere = pl.BlockSpec(memory_space=pl.ANY)
    total = pl.pallas_call(
        kernel,
        out_shape=jax.ShapeDtypeStruct((1, SEQ, EH), F32),
        in_specs=[anywhere, pl.BlockSpec(memory_space=pltpu.SMEM)] + [anywhere] * 5,
        out_specs=pl.BlockSpec(memory_space=pltpu.VMEM),
        scratch_shapes=[
            pltpu.VMEM((2, SEQ, HALF), BF),
            pltpu.VMEM((2, HALF, 3 * HD), BF),
            pltpu.VMEM((2, HD, HALF), BF),
            pltpu.VMEM((HALF, E), BF),
            pltpu.VMEM((CH, SEQ, CW), BF),
            pltpu.VMEM((2, CH, SEQ, CW), BF),
            pltpu.VMEM((2, 2, SEQ, HD), BF),
            pltpu.VMEM((2, PART, E), BF),
            pltpu.VMEM((PART, E), BF),
            pltpu.VMEM((PART, E), BF),
            pltpu.VMEM((2, PART, E), BF),
            pltpu.VMEM((2, PART, E), BF),
            pltpu.VMEM((8, 2, PART // 2, E), BF),
            pltpu.VMEM((8, 2, PART, HD), BF),
            pltpu.VMEM((2, SEQ, HD), BF),
            pltpu.VMEM((2, HD, E), BF),
            pltpu.VMEM((2, HD, E), BF),
            pltpu.VMEM((2, 2, SEQ, EH), F32),
            pltpu.VMEM((2, SEQ, EH), F32),
            pltpu.VMEM((SEQ, EH), BF),
            pltpu.VMEM((SEQ, EH), BF),
            pltpu.SemaphoreType.DMA((9,)),
            pltpu.SemaphoreType.DMA((REMOTES,)),
            pltpu.SemaphoreType.DMA((REMOTES,)),
        ],
        compiler_params=pltpu.CompilerParams(
            collective_id=0, has_side_effects=True, vmem_limit_bytes=60 * 1024 * 1024
        ),
    )(tokens, lengths.reshape(1, SECTIONS), w_query, w_key, w_value, w_out, w_embed)
    return total * (1.0 / (SEQ * GROUPS))


def solution(mesh):
    return jax.shard_map(
        shards,
        mesh=mesh,
        in_specs=(
            P("section", "dp", "tensor"),
            P(None, "dp"),
            P("section", None, "tensor"),
            P("section", None, "tensor"),
            P("section", None, "tensor"),
            P("section", "tensor", None),
            P("tensor", None),
        ),
        out_specs=P("section", "dp", "tensor"),
        check_vma=False,
    )
```
